32 devices in a mesh: groups: 2 (over x), att: 2 (over y), exp: 8 (over z, core).
Axes of the slice: x: 2, y: 2, z: 4, core: 2. Of those that a mesh axis runs over, the one named last changes fastest.
Arguments:
- queries: bfloat16 [1024, 4096], P(('groups', 'exp')), parts along dimension 0, may hold values from -12 to 12
- row_key_value: bfloat16 [1024, 1024], P(('groups', 'exp')), parts along dimension 0, may hold values from -12 to 12
- shared_context_cache: bfloat16 [4, 1024, 1024], P('groups', 'att'), parts along dimension 0, may hold values from -6 to 6
- branch: int32 [1024], P(('groups', 'exp')), parts along dimension 0, may hold values from 0 to 1
- sink_logits: float32 [64], replicated, may hold values from 8 to 13
- w_out: bfloat16 [4096, 2880], P(None, 'att'), may hold values from -0.09375 to 0.09375
- residual: bfloat16 [1024, 2880], P(('groups', 'exp'), 'att'), parts along dimension 0, may hold values from -20 to 20
- norm_gain: bfloat16 [2880], P('att'), may hold values from 0.099609375 to 1.8984375
- expert_ids: int32 [1024, 4], P(('groups', 'exp')), parts along dimension 0, may hold values from 0 to 7, all different within a row; in each aligned block of 64 rows (0 to 63, 64 to 127, ...) at most 64 rows name the same one
- weight_codes: int32 [1024, 4], P(('groups', 'exp')), parts along dimension 0, may hold values from 1 to 255
- w_gate: bfloat16 [8, 2880, 2880], P('exp', None, 'att'), may hold values from -0.4375 to 0.4375
- w_up: bfloat16 [8, 2880, 2880], P('exp', None, 'att'), may hold values from -0.4375 to 0.4375
- w_down: bfloat16 [8, 2880, 2880], P('exp', 'att'), may hold values from -0.013671875 to 0.013671875
Outputs:
- attended: bfloat16 [1024, 2880], P(('groups', 'exp'), 'att'), parts along dimension 0
- expert_mix: bfloat16 [1024, 2880], P(('groups', 'exp'), 'att'), parts along dimension 0
The draws below stay inside these ranges and needn't reach their ends.
There are 2 independent parts, one for each index of `groups`. The reference program is written for one: setup_inputs(seed, part) draws one part's arguments, and reference() takes and returns one part's arrays. A program takes and returns all parts, laid end to end along the dimension named above; an argument that names none is the same for every part. Nothing has to cross between parts.
Inputs may be any that keep to these rules, and one draw needn't show every extreme that they name: `expert_ids`: each row names 4 different experts; within the rows of one index of exp (aligned blocks of 64 rows) no expert is named more than 64 times, and in some block some expert is named exactly 64 times.
All inputs are finite; a program needn't handle non-finite values.
Results may differ from the reference program's by a relative error of at most 0.022.
Values may be sent and summed in bfloat16 or wider, within the bound.
A program may use at most 128 MiB of HBM per device.

```python
import math
from functools import partial
import jax
import jax.numpy as jnp
import numpy as np
from jax import lax

D = 2880
QUERY_HEADS = 64
KEY_VALUE_HEADS = 8
HEAD_SIZE = 64
FF = 2880
TOP = 4
SHARED_CONTEXTS = 2
ROWS_DEV = 64
EXPERTS = 8
DECODE_ROWS = 512
CONTEXT_TOKENS = 1024
CAP = 64
N_EXP = 8


def draw_queries(key, part):
    random_seed_key = jax.random.fold_in(key, 11)
    value_rows = jnp.clip(2.5 * jax.random.normal(random_seed_key, (DECODE_ROWS, QUERY_HEADS, HEAD_SIZE), jnp.float32), -12.0, 12.0)
    return value_rows.reshape(DECODE_ROWS, QUERY_HEADS * HEAD_SIZE).astype(jnp.bfloat16)


def draw_shared_context_cache(key, part):
    random_seed_key = jax.random.fold_in(key, 12)
    value_rows = jnp.clip(jax.random.normal(random_seed_key, (SHARED_CONTEXTS, CONTEXT_TOKENS, 2, KEY_VALUE_HEADS, HEAD_SIZE), jnp.float32), -6.0, 6.0)
    return value_rows.reshape(SHARED_CONTEXTS, CONTEXT_TOKENS, 2 * KEY_VALUE_HEADS * HEAD_SIZE).astype(jnp.bfloat16)


def draw_residual(key, part):
    column = jnp.arange(D, dtype=jnp.float32) / (D - 1)
    random_seed_key = jax.random.fold_in(key, 13)
    value_rows = jnp.clip(jax.random.normal(random_seed_key, (DECODE_ROWS, D), jnp.float32), -6.0, 6.0) * 0.4 * jnp.exp(column * math.log(3.0))[None, :]
    return value_rows.astype(jnp.bfloat16)


def plant(result, own_key, least, largest):
    shape = result.shape
    place = [jax.random.randint(jax.random.fold_in(own_key, axis), (), 0, shape[axis]) for axis in range(len(shape))]
    result = result.at[tuple(place)].set(least)
    longest = shape.index(max(shape))
    place[longest] = (place[longest] + 1) % shape[longest]
    return result.at[tuple(place)].set(largest)


def steps_of(key, extent, cuts, low, high):
    factor_of, own = 1.0, jax.random.fold_in(key, 6)
    for axis_at, parts in cuts:
        steps = jnp.exp(jax.random.uniform(jax.random.fold_in(own, axis_at), (parts,), jnp.float32, low / len(cuts), high / len(cuts)))
        factor_of = factor_of * jnp.repeat(steps, extent[axis_at] // parts).reshape([-1 if axis == axis_at else 1 for axis in range(len(extent))])
    return factor_of


def deal_out(own_key, own, number, rows, amount, top, most, skew):
    order = jax.random.permutation(own_key, amount)
    crowded, usual = load_shares(amount, rows * top, most, skew, True), load_shares(amount, rows * top, most, skew, False)
    places = jnp.arange(amount)

    def named(sizes, turn):
        used = int((sizes > 0).sum())
        fixed = max(1, used // 4)
        passed = fixed + (places - fixed + turn * (used - fixed)) % max(1, amount - fixed)
        return jnp.zeros((amount,), jnp.int32).at[order[jnp.where(places < fixed, places, passed)]].set(jnp.asarray(sizes, jnp.int32))

    sizes = jnp.where(number % 4 == 0, named(crowded, number // 4), named(usual, number - number // 4 - 1))
    mixed = jax.random.permutation(jax.random.fold_in(own, 3), amount)
    donor, taker = mixed[0:amount // 2 * 2:2], mixed[1:amount // 2 * 2:2]
    slack = jnp.minimum(sizes[donor] - 1, most - sizes[taker]) // 2
    slack = jnp.where((donor == order[0]) | (taker == order[0]) | (sizes[taker] == 0), 0, jnp.maximum(slack, 0))
    passed = jax.random.randint(jax.random.fold_in(own, 4), (amount // 2,), 0, 1 << 20) % (slack + 1)
    sizes = sizes.at[donor].add(-passed).at[taker].add(passed)
    labels = jnp.searchsorted(jnp.cumsum(sizes), jnp.arange(rows * top), side="right").astype(jnp.int32)
    listing = labels.reshape(top, rows).T
    listing = listing[jax.random.permutation(jax.random.fold_in(own, 1), rows)]
    turn = jax.random.randint(jax.random.fold_in(own, 2), (rows, 1), 0, top)
    return jnp.take_along_axis(listing, (jnp.arange(top)[None, :] + turn) % top, axis=1)


def load_shares(amount, total, most, skew, full):
    portions = [(1 << 20) // math.isqrt(grade ** skew) + 1 for grade in range(1, amount + 1)]
    largest = most if full else min(most, max(-(-total // amount), total * portions[0] // sum(portions)))
    least = 1 if total - largest >= amount - 1 else 0
    given, rest = [largest] + [least] * (amount - 1), total - largest - least * (amount - 1)
    while rest > 0:
        free = [i for i in range(1, amount) if given[i] < largest] or [i for i in range(1, amount) if given[i] < most]
        mass, left = sum([portions[i] for i in free]), rest
        for i in free:
            extra = min(most - given[i], max(1, left * portions[i] // mass), rest)
            given[i] = given[i] + extra
            rest = rest - extra
    return np.array(given)


def centred(rng, extent, width, bound, cuts=(), kind=jnp.bfloat16):
    loudness = steps_of(rng, extent, cuts, -0.22, 0.18) if cuts else 1.0
    result = jax.random.normal(rng, extent, jnp.float32) * width * loudness
    return jnp.minimum(jnp.maximum(result, -bound), bound).astype(kind)


def setup_inputs(seed: int = 0, part: int = 0) -> dict:
    keys = jax.random.split(jax.random.key(seed), 14)
    part_splits = jax.random.split(jax.random.fold_in(keys[13], part), 14)
    queries = draw_queries(jax.random.fold_in(jax.random.fold_in(keys[13], part), 71), part)
    row_key_value = centred(part_splits[1], (DECODE_ROWS, 2 * KEY_VALUE_HEADS * HEAD_SIZE), 2.0, 12.0, ((0, 8),))
    shared_context_cache = draw_shared_context_cache(jax.random.fold_in(jax.random.fold_in(keys[13], part), 71), part)
    branch = plant(jax.random.randint(part_splits[3], (DECODE_ROWS,), 0, SHARED_CONTEXTS), jax.random.fold_in(part_splits[3], 1), 0, SHARED_CONTEXTS - 1).astype(jnp.int32)
    sink_logits = jnp.clip(jax.random.uniform(keys[4], (QUERY_HEADS,), jnp.float32, 8.0, 13.0), 8.0, 13.0)
    w_out = centred(keys[5], (QUERY_HEADS * HEAD_SIZE, D), (QUERY_HEADS * HEAD_SIZE) ** -0.5, 0.09375, ((1, 2),))
    residual = draw_residual(jax.random.fold_in(jax.random.fold_in(keys[13], part), 71), part)
    norm_gain = jnp.clip(1.0 + 0.18 * jax.random.normal(keys[7], (D,), jnp.float32), 0.099609375, 1.8984375).astype(jnp.bfloat16)
    expert_ids_keys = jax.random.split(jax.random.fold_in(part_splits[8], 1), DECODE_ROWS // ROWS_DEV)
    expert_ids_turns = jax.random.permutation(jax.random.fold_in(part_splits[8], 3), DECODE_ROWS // ROWS_DEV)
    expert_ids = jax.vmap(lambda own, number: deal_out(jax.random.fold_in(part_splits[8], 2), own, number, ROWS_DEV, EXPERTS, TOP, CAP, 2))(expert_ids_keys, expert_ids_turns).reshape((DECODE_ROWS, TOP))
    weight_codes = plant(jax.random.randint(part_splits[9], (DECODE_ROWS, TOP), 1, 256), jax.random.fold_in(part_splits[9], 1), 1, 255).astype(jnp.int32)
    w_gate = centred(keys[10], (EXPERTS, D, FF), (D // 16) ** -0.5, 0.4375, ((0, 8), (2, 2)))
    w_up = centred(keys[11], (EXPERTS, D, FF), (D // 16) ** -0.5, 0.4375, ((0, 8), (2, 2)))
    w_down = centred(keys[12], (EXPERTS, FF, D), (64 * FF) ** -0.5, 0.013671875, ((0, 8), (1, 2)))
    return {"queries": queries, "row_key_value": row_key_value, "shared_context_cache": shared_context_cache, "branch": branch, "sink_logits": sink_logits, "w_out": w_out, "residual": residual, "norm_gain": norm_gain, "expert_ids": expert_ids, "weight_codes": weight_codes, "w_gate": w_gate, "w_up": w_up, "w_down": w_down}


clamp_limit = 7.0

def attend_block(packed, shared_context_cache, sink_logits):
    query_block, fresh_block, block_branch = packed
    decode_row_count = query_block.shape[0]
    heads_per_group = QUERY_HEADS // KEY_VALUE_HEADS
    score_scale = HEAD_SIZE ** (-0.5)
    grouped_heads = query_block.reshape(decode_row_count, KEY_VALUE_HEADS, heads_per_group, HEAD_SIZE).astype(jnp.float32)
    current = None
    for context_slot in range(SHARED_CONTEXTS):
        cached_key_block = shared_context_cache[context_slot, :, :KEY_VALUE_HEADS * HEAD_SIZE].reshape(-1, KEY_VALUE_HEADS, HEAD_SIZE).astype(jnp.float32)
        cached_value_block = shared_context_cache[context_slot, :, KEY_VALUE_HEADS * HEAD_SIZE:].reshape(-1, KEY_VALUE_HEADS, HEAD_SIZE).astype(jnp.float32)
        scores = jnp.einsum('rgqd,tgd->rgqt', grouped_heads, cached_key_block) * score_scale
        local_max = lax.optimization_barrier(jnp.max(scores, axis=-1))
        weights = jnp.exp(scores - local_max[..., None])
        local_total = lax.optimization_barrier(jnp.sum(weights, axis=-1))
        rounded = lax.optimization_barrier(weights.astype(jnp.bfloat16)).astype(jnp.float32)
        local_out = jnp.einsum('rgqt,tgd->rgqd', rounded, cached_value_block)
        if current is None:
            current = (local_max, local_total, local_out)
        else:
            chosen = block_branch == context_slot
            current = (jnp.where(chosen[:, None, None], local_max, current[0]), jnp.where(chosen[:, None, None], local_total, current[1]), jnp.where(chosen[:, None, None, None], local_out, current[2]))
    cache_max = current[0].reshape(decode_row_count, QUERY_HEADS)
    cache_total = current[1].reshape(decode_row_count, QUERY_HEADS)
    cache_out = current[2].reshape(decode_row_count, QUERY_HEADS, HEAD_SIZE)
    row_own_keys = fresh_block[:, :KEY_VALUE_HEADS * HEAD_SIZE].reshape(decode_row_count, KEY_VALUE_HEADS, 1, HEAD_SIZE).astype(jnp.float32)
    row_own_values = fresh_block[:, KEY_VALUE_HEADS * HEAD_SIZE:].reshape(decode_row_count, KEY_VALUE_HEADS, 1, HEAD_SIZE).astype(jnp.float32)
    own_score = (lax.optimization_barrier(jnp.sum(grouped_heads * row_own_keys, axis=-1)) * score_scale).reshape(decode_row_count, QUERY_HEADS)
    row_own_values = jnp.broadcast_to(row_own_values, (decode_row_count, KEY_VALUE_HEADS, heads_per_group, HEAD_SIZE)).reshape(decode_row_count, QUERY_HEADS, HEAD_SIZE)
    sink_row = sink_logits.astype(jnp.float32)[None, :]
    peak = jnp.maximum(jnp.maximum(cache_max, own_score), sink_row)
    cache_factor = jnp.exp(cache_max - peak)
    own_factor = jnp.exp(own_score - peak)
    sink_factor = jnp.exp(sink_row - peak)
    denominator = cache_total * cache_factor + own_factor + sink_factor
    numerator = cache_out * cache_factor[..., None] + own_factor[..., None] * row_own_values
    return (numerator / denominator[..., None]).reshape(decode_row_count, QUERY_HEADS * HEAD_SIZE).astype(jnp.bfloat16)

def reference(queries, row_key_value, shared_context_cache, branch, sink_logits, w_out, residual, norm_gain, expert_ids, weight_codes, w_gate, w_up, w_down):
    total_rows = queries.shape[0]
    blocks = total_rows // ROWS_DEV
    packed = (queries.reshape(blocks, ROWS_DEV, -1), row_key_value.reshape(blocks, ROWS_DEV, -1), branch.reshape(blocks, ROWS_DEV))
    attention = lax.map(partial(attend_block, shared_context_cache=shared_context_cache, sink_logits=sink_logits), packed)
    attention = attention.reshape(total_rows, QUERY_HEADS * HEAD_SIZE)
    hidden = residual.astype(jnp.float32) + jnp.dot(attention, w_out, preferred_element_type=jnp.float32)
    attended = hidden.astype(jnp.bfloat16)
    squares = lax.optimization_barrier(jnp.sum(hidden * hidden, axis=1))
    inverse = lax.rsqrt(squares / D + 1e-05)
    normed = (hidden * inverse[:, None] * norm_gain.astype(jnp.float32)[None, :]).astype(jnp.bfloat16)
    shares = weight_codes.astype(jnp.float32)
    shares = shares / lax.optimization_barrier(jnp.sum(shares, axis=1, keepdims=True))
    room = N_EXP * CAP

    def one_expert(mixture, packed_expert):
        expert, gate_weight, up_weight, down_weight = packed_expert
        expert_hit = expert_ids == expert
        routed = jnp.any(expert_hit, axis=1)
        share = lax.optimization_barrier(jnp.sum(jnp.where(expert_hit, shares, jnp.zeros_like(shares)), axis=1))
        chosen = jnp.nonzero(routed, size=room, fill_value=0)[0].astype(jnp.int32)
        valid = (jnp.arange(room, dtype=jnp.int32) < jnp.sum(routed.astype(jnp.int32))).astype(jnp.float32)
        rows_in = normed[chosen]
        gate_sum = jnp.minimum(jnp.dot(rows_in, gate_weight, preferred_element_type=jnp.float32), clamp_limit)
        up_sum = jnp.clip(jnp.dot(rows_in, up_weight, preferred_element_type=jnp.float32), -clamp_limit, clamp_limit)
        active = (gate_sum * jax.nn.sigmoid(1.702 * gate_sum) * (up_sum + 1.0)).astype(jnp.bfloat16)
        output = jnp.dot(active, down_weight, preferred_element_type=jnp.float32).astype(jnp.bfloat16)
        contribution = output.astype(jnp.float32) * (share[chosen] * valid)[:, None]
        return (mixture.at[chosen].add(contribution), None)
    start_mix = jnp.zeros((total_rows, D), jnp.float32)
    mixture, ignored = lax.scan(one_expert, start_mix, (jnp.arange(EXPERTS, dtype=jnp.int32), w_gate, w_up, w_down))
    return (attended, mixture.astype(jnp.bfloat16))
```

```python
import functools

import jax
import jax.numpy as jnp
from jax import lax
from jax.experimental import pallas as pl
from jax.experimental.pallas import tpu as pltpu
from jax.sharding import PartitionSpec as P

D = 2880
QUERY_HEADS = 64
KEY_VALUE_HEADS = 8
HEAD_SIZE = 64
TOP = 4
SHARED_CONTEXTS = 2


MESH = pl.DeviceIdType.MESH
NT = (((1,), (1,)), ((), ()))
clamp_limit = 7.0


def combined_all(x, axis, combine):
    everything = jax.tree.map(
        lambda part, kind: lax.all_gather(part.astype(kind), axis),
        x,
        jax.tree.map(lambda a: jnp.bfloat16 if a.dtype == jnp.float32 else a.dtype, x),
    )

    def take(k):
        return jax.tree.map(lambda part, own: part[k].astype(own.dtype), everything, x)

    return lax.fori_loop(
        1, lax.axis_size(axis), lambda k, so_far: combine(so_far, take(k)), take(0)
    )


def merge_parts(first, second):
    first_max, first_total, first_out = first
    second_max, second_total, second_out = second
    joint_max = jnp.maximum(first_max, second_max)
    first_factor = jnp.exp(first_max - joint_max)
    second_factor = jnp.exp(second_max - joint_max)
    joint_total = first_total * first_factor + second_total * second_factor
    decode_row_count, head_count = first_max.shape
    joint_out = (
        first_out.reshape(decode_row_count, head_count, -1) * first_factor[:, :, None]
        + second_out.reshape(decode_row_count, head_count, -1) * second_factor[:, :, None]
    )
    return (joint_max, joint_total, joint_out.reshape(decode_row_count, -1))


def local_partials(grouped_heads, shared_context_cache, branch):
    decode_row_count = grouped_heads.shape[0]
    score_scale = HEAD_SIZE ** (-0.5)
    current = None
    for context_slot in range(SHARED_CONTEXTS):
        cached_key_block = shared_context_cache[
            context_slot, :, : KEY_VALUE_HEADS * HEAD_SIZE
        ].reshape(-1, KEY_VALUE_HEADS, HEAD_SIZE)
        cached_value_block = shared_context_cache[
            context_slot, :, KEY_VALUE_HEADS * HEAD_SIZE :
        ].reshape(-1, KEY_VALUE_HEADS, HEAD_SIZE)
        scores = (
            jnp.einsum(
                "rgqd,tgd->rgqt",
                grouped_heads,
                cached_key_block,
                preferred_element_type=jnp.float32,
            )
            * score_scale
        )
        local_max = jnp.max(scores, axis=-1)
        weights = jnp.exp(scores - local_max[..., None])
        local_total = jnp.sum(weights, axis=-1)
        local_out = jnp.einsum(
            "rgqt,tgd->rgqd",
            weights.astype(jnp.bfloat16),
            cached_value_block,
            preferred_element_type=jnp.float32,
        )
        if current is None:
            current = (local_max, local_total, local_out)
        else:
            chosen = branch == context_slot
            current = (
                jnp.where(chosen[:, None, None], local_max, current[0]),
                jnp.where(chosen[:, None, None], local_total, current[1]),
                jnp.where(chosen[:, None, None, None], local_out, current[2]),
            )
    return (
        current[0].reshape(decode_row_count, QUERY_HEADS),
        current[1].reshape(decode_row_count, QUERY_HEADS),
        current[2].reshape(decode_row_count, QUERY_HEADS * HEAD_SIZE),
    )


def finish_attention(merged, grouped_heads, row_key_value, sink_logits):
    decode_row_count = grouped_heads.shape[0]
    heads_per_group = QUERY_HEADS // KEY_VALUE_HEADS
    score_scale = HEAD_SIZE ** (-0.5)
    cache_max, cache_total, cache_out = merged
    row_own_keys = (
        row_key_value[:, : KEY_VALUE_HEADS * HEAD_SIZE]
        .reshape(decode_row_count, KEY_VALUE_HEADS, 1, HEAD_SIZE)
        .astype(jnp.float32)
    )
    row_own_values = (
        row_key_value[:, KEY_VALUE_HEADS * HEAD_SIZE :]
        .reshape(decode_row_count, KEY_VALUE_HEADS, 1, HEAD_SIZE)
        .astype(jnp.float32)
    )
    own_score = (
        jnp.sum(grouped_heads.astype(jnp.float32) * row_own_keys, axis=-1) * score_scale
    ).reshape(decode_row_count, QUERY_HEADS)
    row_own_values = jnp.broadcast_to(
        row_own_values, (decode_row_count, KEY_VALUE_HEADS, heads_per_group, HEAD_SIZE)
    ).reshape(decode_row_count, QUERY_HEADS, HEAD_SIZE)
    sink_row = sink_logits[None, :]
    peak = jnp.maximum(jnp.maximum(cache_max, own_score), sink_row)
    cache_factor = jnp.exp(cache_max - peak)
    own_factor = jnp.exp(own_score - peak)
    sink_factor = jnp.exp(sink_row - peak)
    denominator = cache_total * cache_factor + own_factor + sink_factor
    numerator = (
        cache_out.reshape(decode_row_count, QUERY_HEADS, HEAD_SIZE) * cache_factor[..., None]
        + own_factor[..., None] * row_own_values
    )
    return (
        (numerator / denominator[..., None])
        .reshape(decode_row_count, QUERY_HEADS * HEAD_SIZE)
        .astype(jnp.bfloat16)
    )

def layer_kernel(
    n,
    q_ref,
    kv_ref,
    branch_ref,
    sink_ref,
    residual_ref,
    gain_ref,
    ids_ref,
    codes_ref,
    cache_hbm,
    wo_hbm,
    wg_hbm,
    wu_hbm,
    wd_hbm,
    attended_ref,
    out_ref,
    cache,
    wo,
    hidden_t,
    OS,
    OR,
    TS,
    TR,
    osend,
    orecv,
    tsend,
    trecv,
    wg,
    wu,
    wd,
    X,
    act_ref,
    PS,
    CS,
    KEEP,
    YS,
    YR,
    ZS,
    ZR,
    wsem,
    xysend,
    xzsend,
    xmsend,
    xrecv,
    csend,
    crecv,
    ysend,
    yrecv,
    zsend,
    zrecv,
):
    rings = n // 2
    rows = residual_ref.shape[0]
    width = residual_ref.shape[1]
    half = X.shape[4]
    parts = rows // half
    experts = n
    a = lax.axis_index("att")
    e = lax.axis_index("exp")
    z = e // 2
    c = e % 2

    upper = z // 2
    twin = upper * 2 + 1 - z % 2
    near = 2 - upper
    far = 3 * (1 - upper)
    others = [twin, near, far]
    mate = {"exp": z * 2 + 1 - c}
    across = {"att": 1 - a}

    cache_load = pltpu.make_async_copy(cache_hbm, cache, wsem.at[3])
    cache_load.start()
    wo_load = pltpu.make_async_copy(wo_hbm, wo, wsem.at[4])
    wo_load.start()
    loads = [
        pltpu.make_async_copy(wg_hbm.at[0], wg, wsem.at[0]),
        pltpu.make_async_copy(wu_hbm.at[0], wu, wsem.at[1]),
        pltpu.make_async_copy(wd_hbm.at[0], wd, wsem.at[2]),
    ]
    for load in loads:
        load.start()

    barrier = pltpu.get_barrier_semaphore()
    for target in [mate, across] + [{"exp": chip * 2 + c} for chip in others]:
        pl.semaphore_signal(barrier, inc=1, device_id=target, device_id_type=MESH)
    pl.semaphore_wait(barrier, 2 + len(others))
    eye = lax.broadcasted_iota(jnp.int32, (rows, rows), 0) == lax.broadcasted_iota(
        jnp.int32, (rows, rows), 1
    )

    per = QUERY_HEADS // KEY_VALUE_HEADS
    columns = per * rows
    pair = 2 * HEAD_SIZE
    pairs = KEY_VALUE_HEADS // 2
    kv_width = KEY_VALUE_HEADS * HEAD_SIZE
    second_context = jnp.concatenate([branch_ref[...]] * per, axis=1) == 1

    def transposed_queries(g2):
        start = pl.multiple_of(g2 * 2 * per * HEAD_SIZE, 128)
        block = q_ref[:, pl.ds(start, 2 * per * HEAD_SIZE)].astype(jnp.float32).T
        block = block * HEAD_SIZE ** (-0.5)

        def head(k):
            return block[k * HEAD_SIZE : (k + 1) * HEAD_SIZE]

        return [
            jnp.concatenate([head(j * per + h) for h in range(per)], axis=1) for j in range(2)
        ]

    def parts_copies(g2):
        return (
            pltpu.make_async_remote_copy(
                src_ref=OS.at[g2],
                dst_ref=OR.at[g2],
                send_sem=osend.at[g2],
                recv_sem=orecv.at[g2],
                device_id=across,
                device_id_type=MESH,
            ),
            pltpu.make_async_remote_copy(
                src_ref=TS.at[g2],
                dst_ref=TR.at[g2],
                send_sem=tsend.at[g2],
                recv_sem=trecv.at[g2],
                device_id=across,
                device_id_type=MESH,
            ),
        )

    cache_load.wait()

    @pl.loop(0, pairs)
    def _(g2):
        heads_t = transposed_queries(g2)
        key_cols = pl.ds(pl.multiple_of(g2 * pair, 128), pair)
        value_cols = pl.ds(pl.multiple_of(kv_width + g2 * pair, 128), pair)
        keys = jnp.concatenate([cache[0, :, key_cols], cache[1, :, key_cols]], axis=1)
        values_t = [cache[k, :, value_cols].T for k in range(2)]
        for j in range(2):
            q = heads_t[j]
            none = jnp.zeros_like(q)
            first_q = jnp.where(second_context, 0.0, q)
            second_q = jnp.where(second_context, q, 0.0)
            stack = [first_q, none, second_q, none] if j == 0 else [none, first_q, none, second_q]
            stacked = jnp.concatenate(stack, axis=0).astype(jnp.bfloat16)
            scores = jnp.dot(keys, stacked, preferred_element_type=jnp.float32)
            top = jnp.max(scores, axis=0, keepdims=True)
            weights = jnp.exp(scores - top)
            total = jnp.sum(weights, axis=0, keepdims=True)
            own_rows = slice(j * HEAD_SIZE, (j + 1) * HEAD_SIZE)
            values = jnp.concatenate([v[own_rows] for v in values_t], axis=0)
            out = jnp.dot(
                values, weights.astype(jnp.bfloat16), preferred_element_type=jnp.float32
            )
            out = jnp.where(second_context, out[HEAD_SIZE:], out[:HEAD_SIZE])
            OS[g2, own_rows, :] = out.astype(jnp.bfloat16)
            TS[g2, 2 * j : 2 * j + 1, :] = top
            TS[g2, 2 * j + 1 : 2 * j + 2, :] = total
        for copy in parts_copies(g2):
            copy.start()

    hidden_t[...] = jnp.zeros_like(hidden_t)
    wo_load.wait()

    @pl.loop(0, pairs)
    def _(g2):
        heads_t = transposed_queries(g2)
        key_cols = pl.ds(pl.multiple_of(g2 * pair, 128), pair)
        value_cols = pl.ds(pl.multiple_of(kv_width + g2 * pair, 128), pair)
        own_keys = kv_ref[:, key_cols].astype(jnp.float32).T
        own_values = kv_ref[:, value_cols].astype(jnp.float32).T
        for copy in parts_copies(g2):
            copy.wait()
        mine, theirs = TS[g2], TR[g2]
        stacked = []
        for j in range(2):
            own_rows = slice(j * HEAD_SIZE, (j + 1) * HEAD_SIZE)
            own_key = jnp.concatenate([own_keys[own_rows]] * per, axis=1)
            own_value = jnp.concatenate([own_values[own_rows]] * per, axis=1)
            own_score = jnp.sum(heads_t[j] * own_key, axis=0, keepdims=True)
            sink = jnp.concatenate(
                [jnp.full((1, rows), sink_ref[(g2 * 2 + j) * per + h]) for h in range(per)], axis=1
            )
            top_a, top_b = mine[2 * j : 2 * j + 1], theirs[2 * j : 2 * j + 1]
            peak = jnp.maximum(jnp.maximum(top_a, top_b), jnp.maximum(own_score, sink))
            factor_a = jnp.exp(top_a - peak)
            factor_b = jnp.exp(top_b - peak)
            own_factor = jnp.exp(own_score - peak)
            denominator = (
                mine[2 * j + 1 : 2 * j + 2] * factor_a
                + theirs[2 * j + 1 : 2 * j + 2] * factor_b
                + own_factor
                + jnp.exp(sink - peak)
            )
            out = (
                OS[g2, own_rows, :].astype(jnp.float32) * factor_a
                + OR[g2, own_rows, :].astype(jnp.float32) * factor_b
                + own_factor * own_value
            ) / denominator
            stacked += [out[:, h * rows : (h + 1) * rows] for h in range(per)]
        attention_t = jnp.concatenate(stacked, axis=0).astype(jnp.bfloat16)
        cols = pl.ds(pl.multiple_of(g2 * 2 * per * HEAD_SIZE, 128), 2 * per * HEAD_SIZE)
        hidden_t[...] += jnp.dot(wo[:, cols], attention_t, preferred_element_type=jnp.float32)

    hidden = hidden_t[...].T + residual_ref[...].astype(jnp.float32)
    attended_ref[...] = hidden.astype(jnp.bfloat16)
    squares = jnp.sum(hidden * hidden, axis=1, keepdims=True)
    codes = codes_ref[...].astype(jnp.float32)
    codes = codes / jnp.sum(codes, axis=0, keepdims=True)
    row_of = lax.broadcasted_iota(jnp.int32, (experts, rows), 0)
    table = jnp.zeros((experts, rows), jnp.float32)
    for k in range(TOP):
        table += jnp.where(row_of == ids_ref[k : k + 1, :], codes[k : k + 1, :], 0.0)
    high = table.astype(jnp.bfloat16)
    low = (table - high.astype(jnp.float32)).astype(jnp.bfloat16)
    upright = lax.dot_general(
        eye.astype(jnp.bfloat16),
        jnp.concatenate([high, low], axis=0),
        NT,
        preferred_element_type=jnp.float32,
    )
    first_part = squares.astype(jnp.bfloat16).astype(jnp.float32)
    second_part = (squares - first_part).astype(jnp.bfloat16).astype(jnp.float32)
    third_part = squares - first_part - second_part
    spare = X.shape[5] - width
    notes = jnp.concatenate(
        [
            upright,
            first_part,
            second_part,
            third_part,
            jnp.zeros((rows, spare - 2 * experts - 3), jnp.float32),
        ],
        axis=1,
    )
    scaled = jnp.concatenate([hidden * gain_ref[...].astype(jnp.float32), notes], axis=1)
    scaled = scaled.astype(jnp.bfloat16)
    for h in range(parts):
        X[a, h, c, z] = scaled[h * half : (h + 1) * half]

    pending = []

    def push(ref, index, target, sent, received):
        copy = pltpu.make_async_remote_copy(
            src_ref=ref.at[index],
            dst_ref=ref.at[index],
            send_sem=sent,
            recv_sem=received,
            device_id=target,
            device_id_type=MESH,
        )
        copy.start()
        pending.append(copy)

    def arrived(side, h, core, chip):
        pltpu.make_async_remote_copy(
            src_ref=X.at[side, h, core, chip],
            dst_ref=X.at[side, h, core, chip],
            send_sem=xmsend.at[0],
            recv_sem=xrecv.at[side, h, core, chip],
            device_id=mate,
            device_id_type=MESH,
        ).wait_recv()

    def to_mate(side, h, chip, slot):
        push(
            X, (side, h, c, chip), mate, xmsend.at[slot], xrecv.at[side, h, c, chip]
        )

    def to_across(h, chip, slot):
        push(X, (a, h, c, chip), across, xysend.at[slot], xrecv.at[a, h, c, chip])

    order = [z] + others

    def came(h, k):
        arrived(a, h, c, order[k])
        to_across(h, order[k], h * rings + k)
        to_mate(a, h, order[k], (h * 2) * rings + k)

    def crossed(h, k):
        arrived(1 - a, h, c, order[k])
        to_mate(1 - a, h, order[k], (h * 2 + 1) * rings + k)

    def mates(h):
        for chip in order:
            for side in range(2):
                arrived(side, h, 1 - c, chip)

    for h in range(parts):
        to_across(h, z, h * rings)
        for k in (3, 2, 1):
            push(
                X,
                (a, h, c, z),
                {"exp": order[k] * 2 + c},
                xzsend.at[h * rings + k],
                xrecv.at[a, h, c, z],
            )
        to_mate(a, h, z, (h * 2) * rings)

    count = n * half

    def tiles_of(total, tile):
        return [(start, min(tile, total - start)) for start in range(0, total, tile)]

    def prepare(h):
        sides = [X[side, h].reshape(count, X.shape[5]) for side in range(2)]
        x = jnp.concatenate([side[:, :width] for side in sides], axis=1)
        notes = [side[:, width:].astype(jnp.float32) for side in sides]
        lane = lax.broadcasted_iota(jnp.int32, notes[0].shape, 1)
        mine = (lane == e) | (lane == e + experts)
        share = jnp.sum(jnp.where(mine, notes[0], 0.0), axis=1, keepdims=True)
        sums = (lane >= 2 * experts) & (lane < 2 * experts + 3)
        squares = jnp.sum(
            jnp.where(sums, notes[0] + notes[1], 0.0), axis=1, keepdims=True
        )
        return x, share, lax.rsqrt(squares / (2 * width) + 1e-05)

    def first(x, inverse, start, size):
        cols = pl.ds(start, size)
        g = lax.dot_general(x, wg[cols, :], NT, preferred_element_type=jnp.float32)
        u = lax.dot_general(x, wu[cols, :], NT, preferred_element_type=jnp.float32)
        g = jnp.minimum(g * inverse, clamp_limit)
        u = jnp.clip(u * inverse, -clamp_limit, clamp_limit)
        act_ref[:, cols] = (g * jax.nn.sigmoid(1.702 * g) * (u + 1.0)).astype(jnp.bfloat16)

    lead = width % 128
    reach = width + lead

    def second(share, s):
        side = (1 - a) if s == 0 else a
        cols = pl.ds(pl.multiple_of(side * (width - lead), 128), reach)
        y = jnp.dot(act_ref[...], wd[:, cols], preferred_element_type=jnp.float32)
        y = jnp.where(side == 0, y[:, :width], y[:, lead:]) * share
        y = y.astype(jnp.bfloat16)
        for k in range(2):
            PS[s, k] = y[k * rings * half : (k + 1) * rings * half]

    def swap(h, s):
        copy = pltpu.make_async_remote_copy(
            src_ref=PS.at[s, 1 - c],
            dst_ref=CS.at[h, s],
            send_sem=csend.at[h, s],
            recv_sem=crecv.at[h, s],
            device_id=mate,
            device_id_type=MESH,
        )
        copy.start()
        return copy

    def chip_rows(chip):
        return pl.ds(pl.multiple_of(chip * half, half), half)

    def cross_over(h):
        total = PS[0, c].astype(jnp.float32) + CS[h, 0].astype(jnp.float32)
        YS[h] = total.astype(jnp.bfloat16)
        copies = []
        for k in (3, 2, 1, 0):
            copy = pltpu.make_async_remote_copy(
                src_ref=YS.at[h, chip_rows(order[k])],
                dst_ref=YR.at[h, chip_rows(order[k])],
                send_sem=ysend.at[h, k],
                recv_sem=yrecv.at[h, k],
                device_id=across,
                device_id_type=MESH,
            )
            copy.start()
            copies.append(copy)
        return copies[::-1]

    def keep(h):
        KEEP[h] = PS[1, c].astype(jnp.float32) + CS[h, 1].astype(jnp.float32)

    def deliver(h, k, crossing):
        crossing[k].wait()
        mine = chip_rows(order[k])
        total = KEEP[h, mine] + YR[h, mine].astype(jnp.float32)
        ZS[h, mine] = total.astype(jnp.bfloat16)
        copy = pltpu.make_async_remote_copy(
            src_ref=ZS.at[h, mine],
            dst_ref=ZR.at[h, z],
            send_sem=zsend.at[h, k],
            recv_sem=zrecv.at[h, z],
            device_id={"exp": order[k] * 2 + c},
            device_id_type=MESH,
        )
        copy.start()
        pending.append(copy)

    def finish(h, crossing):
        crossing[0].wait()
        mine = chip_rows(z)
        total = KEEP[h, mine] + YR[h, mine].astype(jnp.float32)
        for k in (1, 2, 3):
            pltpu.make_async_remote_copy(
                src_ref=ZR.at[h, order[k]],
                dst_ref=ZR.at[h, order[k]],
                send_sem=zsend.at[h, 0],
                recv_sem=zrecv.at[h, order[k]],
                device_id=mate,
                device_id_type=MESH,
            ).wait_recv()
            total += ZR[h, order[k]].astype(jnp.float32)
        out_ref[h * half : (h + 1) * half, :] = total.astype(jnp.bfloat16)

    came(0, 1)
    crossed(0, 0)
    came(0, 2)
    crossed(0, 1)
    came(0, 3)
    crossed(0, 2)
    crossed(0, 3)
    mates(0)
    loads[0].wait()
    loads[1].wait()
    x, share, inverse = prepare(0)
    came(1, 1)
    crossed(1, 0)
    tiles = tiles_of(width, 512)
    first(x, inverse, *tiles[0])
    came(1, 2)
    first(x, inverse, *tiles[1])
    crossed(1, 1)
    for tile in tiles[2:]:
        first(x, inverse, *tile)
    came(1, 3)
    crossed(1, 2)
    loads[2].wait()
    second(share, 0)
    swap_other = swap(0, 0)
    second(share, 1)
    swap_own = swap(0, 1)
    swap_other.wait()
    crossing_0 = cross_over(0)
    crossed(1, 3)
    swap_own.wait()
    keep(0)
    mates(1)
    x, share, inverse = prepare(1)
    first(x, inverse, *tiles[0])
    first(x, inverse, *tiles[1])
    deliver(0, 3, crossing_0)
    for tile in tiles[2:]:
        first(x, inverse, *tile)
    deliver(0, 2, crossing_0)
    second(share, 0)
    swap_other = swap(1, 0)
    deliver(0, 1, crossing_0)
    second(share, 1)
    swap_own = swap(1, 1)
    swap_other.wait()
    crossing_1 = cross_over(1)
    swap_own.wait()
    keep(1)
    finish(0, crossing_0)
    for k in (3, 2, 1):
        deliver(1, k, crossing_1)
    finish(1, crossing_1)
    for copy in pending:
        copy.wait_send()


def layer(
    queries, row_key_value, cache, branch, sinks, w_out, residual, gain, expert_ids, weight_codes, w_gate, w_up, w_down
):
    n = lax.axis_size("exp")
    rings = n // 2
    rows, width = residual.shape
    per = QUERY_HEADS // KEY_VALUE_HEADS
    pairs = KEY_VALUE_HEADS // 2
    full = 2 * width
    half = rows // 2
    wide = -(-width // 128) * 128
    block = rings * half
    bf = jnp.bfloat16
    dma = pltpu.SemaphoreType.DMA
    return pl.pallas_call(
        functools.partial(layer_kernel, n),
        out_shape=[jax.ShapeDtypeStruct((rows, width), bf)] * 2,
        in_specs=[pl.BlockSpec(memory_space=pltpu.VMEM)] * 3
        + [pl.BlockSpec(memory_space=pltpu.SMEM)]
        + [pl.BlockSpec(memory_space=pltpu.VMEM)] * 4
        + [pl.BlockSpec(memory_space=pl.ANY)] * 5,
        out_specs=[pl.BlockSpec(memory_space=pltpu.VMEM)] * 2,
        scratch_shapes=[
            pltpu.VMEM(cache.shape, bf),
            pltpu.VMEM((width, QUERY_HEADS * HEAD_SIZE), bf),
            pltpu.VMEM((width, rows), jnp.float32),
            pltpu.VMEM((pairs, 2 * HEAD_SIZE, per * rows), bf),
            pltpu.VMEM((pairs, 2 * HEAD_SIZE, per * rows), bf),
            pltpu.VMEM((pairs, 8, per * rows), jnp.float32),
            pltpu.VMEM((pairs, 8, per * rows), jnp.float32),
            dma((pairs,)),
            dma((pairs,)),
            dma((pairs,)),
            dma((pairs,)),
            pltpu.VMEM((width, full), bf),
            pltpu.VMEM((width, full), bf),
            pltpu.VMEM((width, full), bf),
            pltpu.VMEM((2, 2, 2, rings, half, wide), bf),
            pltpu.VMEM((n * half, width), bf),
            pltpu.VMEM((2, 2, block, width), bf),
            pltpu.VMEM((2, 2, block, width), bf),
            pltpu.VMEM((2, block, width), jnp.float32),
            pltpu.VMEM((2, block, width), bf),
            pltpu.VMEM((2, block, width), bf),
            pltpu.VMEM((2, block, width), bf),
            pltpu.VMEM((2, rings, half, width), bf),
            dma((5,)),
            dma((2 * rings,)),
            dma((2 * rings,)),
            dma((4 * rings,)),
            dma((2, 2, 2, rings)),
            dma((2, 2)),
            dma((2, 2)),
            dma((2, rings)),
            dma((2, rings)),
            dma((2, rings)),
            dma((2, rings)),
        ],
        compiler_params=pltpu.CompilerParams(
            collective_id=1, has_side_effects=True, vmem_limit_bytes=62 * 1024 * 1024
        ),
    )(
        queries,
        row_key_value,
        branch[None, :],
        sinks,
        residual,
        gain[None, :],
        expert_ids.T,
        weight_codes.T,
        cache,
        w_out.T,
        jnp.swapaxes(w_gate, 1, 2),
        jnp.swapaxes(w_up, 1, 2),
        w_down,
    )


def routed_experts(hidden, norm_gain, expert_ids, weight_codes, w_gate, w_up, w_down):
    decode_row_count = hidden.shape[0]
    squares = lax.psum(jnp.sum(hidden * hidden, axis=1), "att")
    inverse = lax.rsqrt(squares / D + 1e-05)
    normed = (hidden * inverse[:, None] * norm_gain.astype(jnp.float32)[None, :]).astype(
        jnp.bfloat16
    )
    local_experts = w_gate.shape[0]
    expert_count = local_experts * lax.axis_size("exp")
    capacity = min(decode_row_count, max(2, 2 * decode_row_count * TOP // expert_count))
    flat_ids = expert_ids.reshape(-1)
    expert_hits = (flat_ids[:, None] == jnp.arange(expert_count, dtype=jnp.int32)[None, :]).astype(
        jnp.int32
    )
    entries = flat_ids.shape[0]
    before = jnp.arange(entries)[:, None] > jnp.arange(entries)[None, :]
    earlier = jnp.dot(
        before.astype(jnp.bfloat16),
        expert_hits.astype(jnp.bfloat16),
        preferred_element_type=jnp.float32,
    ).astype(jnp.int32)
    position = jnp.sum(earlier * expert_hits, axis=1)
    slot_index = flat_ids * capacity + position
    placed = slot_index[None, :] == jnp.arange(expert_count * capacity, dtype=jnp.int32)[:, None]
    assign = jnp.any(placed.reshape(expert_count * capacity, decode_row_count, TOP), axis=2).astype(
        jnp.bfloat16
    )
    source_rows = lax.all_gather(normed, "att", axis=1, tiled=True)
    outgoing = jnp.dot(assign, source_rows, preferred_element_type=jnp.float32).astype(jnp.bfloat16)
    outgoing = outgoing.reshape(expert_count, capacity, -1)
    received = lax.all_to_all(outgoing, "exp", split_axis=0, concat_axis=0, tiled=True)
    senders = received.shape[0] // local_experts
    slot_count = received.shape[1]
    arranged = received.reshape(senders, local_experts, slot_count, received.shape[2])
    gate_sum = jnp.einsum("sekd,edf->sekf", arranged, w_gate, preferred_element_type=jnp.float32)
    up_sum = jnp.einsum("sekd,edf->sekf", arranged, w_up, preferred_element_type=jnp.float32)
    gate_sum = jnp.minimum(gate_sum, clamp_limit)
    up_sum = jnp.clip(up_sum, -clamp_limit, clamp_limit)
    active = (gate_sum * jax.nn.sigmoid(1.702 * gate_sum) * (up_sum + 1.0)).astype(jnp.bfloat16)
    partial_out = jnp.einsum("sekf,efd->sekd", active, w_down, preferred_element_type=jnp.float32)
    summed = lax.psum_scatter(
        partial_out.astype(jnp.bfloat16), "att", scatter_dimension=3, tiled=True
    )
    answer = lax.all_to_all(
        summed.reshape(senders * local_experts, slot_count, -1),
        "exp",
        split_axis=0,
        concat_axis=0,
        tiled=True,
    )
    flat_returned = answer.reshape(expert_count * capacity, -1)
    picked = flat_returned[slot_index].reshape(decode_row_count, TOP, -1).astype(jnp.float32)
    shares = weight_codes.astype(jnp.float32)
    shares = shares / jnp.sum(shares, axis=1, keepdims=True)
    mixture = jnp.sum(picked * shares[:, :, None], axis=1).astype(jnp.bfloat16)
    return mixture


def shards(
    queries,
    row_key_value,
    shared_context_cache,
    branch,
    sink_logits,
    w_out,
    residual,
    norm_gain,
    expert_ids,
    weight_codes,
    w_gate,
    w_up,
    w_down,
):
    near = lax.axis_size("att") == 2 and lax.axis_size("exp") == 8 and w_gate.shape[0] == 1
    if near:
        return layer(
            queries,
            row_key_value,
            shared_context_cache,
            branch,
            sink_logits,
            w_out,
            residual,
            norm_gain,
            expert_ids,
            weight_codes,
            w_gate,
            w_up,
            w_down,
        )
    decode_row_count = queries.shape[0]
    grouped_heads = queries.reshape(
        decode_row_count, KEY_VALUE_HEADS, QUERY_HEADS // KEY_VALUE_HEADS, HEAD_SIZE
    )
    partial_stats = local_partials(grouped_heads, shared_context_cache, branch)
    merged = combined_all(partial_stats, "att", merge_parts)
    attention = finish_attention(merged, grouped_heads, row_key_value, sink_logits)
    projected = jnp.dot(attention, w_out, preferred_element_type=jnp.float32)
    hidden = residual.astype(jnp.float32) + projected
    attended = hidden.astype(jnp.bfloat16)
    mixture = routed_experts(
        hidden, norm_gain, expert_ids, weight_codes, w_gate, w_up, w_down
    )
    return (attended, mixture)


def solution(mesh):
    placed = (
        P(("groups", "exp"), None),
        P(("groups", "exp"), None),
        P("groups", "att", None),
        P(("groups", "exp")),
        P(),
        P(None, "att"),
        P(("groups", "exp"), "att"),
        P("att"),
        P(("groups", "exp"), None),
        P(("groups", "exp"), None),
        P("exp", None, "att"),
        P("exp", None, "att"),
        P("exp", "att", None),
    )
    return jax.shard_map(
        shards,
        mesh=mesh,
        in_specs=placed,
        out_specs=(P(("groups", "exp"), "att"), P(("groups", "exp"), "att")),
        check_vma=False,
    )
```

```python
import functools

import jax
import jax.numpy as jnp
from jax import lax
from jax.experimental import pallas as pl
from jax.experimental.pallas import tpu as pltpu
from jax.sharding import PartitionSpec as P

D = 2880
QUERY_HEADS = 64
KEY_VALUE_HEADS = 8
HEAD_SIZE = 64
TOP = 4
SHARED_CONTEXTS = 2


MESH = pl.DeviceIdType.MESH
NT = (((1,), (1,)), ((), ()))
clamp_limit = 7.0


def combined_all(x, axis, combine):
    everything = jax.tree.map(
        lambda part, kind: lax.all_gather(part.astype(kind), axis),
        x,
        jax.tree.map(lambda a: jnp.bfloat16 if a.dtype == jnp.float32 else a.dtype, x),
    )

    def take(k):
        return jax.tree.map(lambda part, own: part[k].astype(own.dtype), everything, x)

    return lax.fori_loop(
        1, lax.axis_size(axis), lambda k, so_far: combine(so_far, take(k)), take(0)
    )


def merge_parts(first, second):
    first_max, first_total, first_out = first
    second_max, second_total, second_out = second
    joint_max = jnp.maximum(first_max, second_max)
    first_factor = jnp.exp(first_max - joint_max)
    second_factor = jnp.exp(second_max - joint_max)
    joint_total = first_total * first_factor + second_total * second_factor
    decode_row_count, head_count = first_max.shape
    joint_out = (
        first_out.reshape(decode_row_count, head_count, -1) * first_factor[:, :, None]
        + second_out.reshape(decode_row_count, head_count, -1) * second_factor[:, :, None]
    )
    return (joint_max, joint_total, joint_out.reshape(decode_row_count, -1))


def local_partials(grouped_heads, shared_context_cache, branch):
    decode_row_count = grouped_heads.shape[0]
    score_scale = HEAD_SIZE ** (-0.5)
    current = None
    for context_slot in range(SHARED_CONTEXTS):
        cached_key_block = shared_context_cache[
            context_slot, :, : KEY_VALUE_HEADS * HEAD_SIZE
        ].reshape(-1, KEY_VALUE_HEADS, HEAD_SIZE)
        cached_value_block = shared_context_cache[
            context_slot, :, KEY_VALUE_HEADS * HEAD_SIZE :
        ].reshape(-1, KEY_VALUE_HEADS, HEAD_SIZE)
        scores = (
            jnp.einsum(
                "rgqd,tgd->rgqt",
                grouped_heads,
                cached_key_block,
                preferred_element_type=jnp.float32,
            )
            * score_scale
        )
        local_max = jnp.max(scores, axis=-1)
        weights = jnp.exp(scores - local_max[..., None])
        local_total = jnp.sum(weights, axis=-1)
        local_out = jnp.einsum(
            "rgqt,tgd->rgqd",
            weights.astype(jnp.bfloat16),
            cached_value_block,
            preferred_element_type=jnp.float32,
        )
        if current is None:
            current = (local_max, local_total, local_out)
        else:
            chosen = branch == context_slot
            current = (
                jnp.where(chosen[:, None, None], local_max, current[0]),
                jnp.where(chosen[:, None, None], local_total, current[1]),
                jnp.where(chosen[:, None, None, None], local_out, current[2]),
            )
    return (
        current[0].reshape(decode_row_count, QUERY_HEADS),
        current[1].reshape(decode_row_count, QUERY_HEADS),
        current[2].reshape(decode_row_count, QUERY_HEADS * HEAD_SIZE),
    )


def finish_attention(merged, grouped_heads, row_key_value, sink_logits):
    decode_row_count = grouped_heads.shape[0]
    heads_per_group = QUERY_HEADS // KEY_VALUE_HEADS
    score_scale = HEAD_SIZE ** (-0.5)
    cache_max, cache_total, cache_out = merged
    row_own_keys = (
        row_key_value[:, : KEY_VALUE_HEADS * HEAD_SIZE]
        .reshape(decode_row_count, KEY_VALUE_HEADS, 1, HEAD_SIZE)
        .astype(jnp.float32)
    )
    row_own_values = (
        row_key_value[:, KEY_VALUE_HEADS * HEAD_SIZE :]
        .reshape(decode_row_count, KEY_VALUE_HEADS, 1, HEAD_SIZE)
        .astype(jnp.float32)
    )
    own_score = (
        jnp.sum(grouped_heads.astype(jnp.float32) * row_own_keys, axis=-1) * score_scale
    ).reshape(decode_row_count, QUERY_HEADS)
    row_own_values = jnp.broadcast_to(
        row_own_values, (decode_row_count, KEY_VALUE_HEADS, heads_per_group, HEAD_SIZE)
    ).reshape(decode_row_count, QUERY_HEADS, HEAD_SIZE)
    sink_row = sink_logits[None, :]
    peak = jnp.maximum(jnp.maximum(cache_max, own_score), sink_row)
    cache_factor = jnp.exp(cache_max - peak)
    own_factor = jnp.exp(own_score - peak)
    sink_factor = jnp.exp(sink_row - peak)
    denominator = cache_total * cache_factor + own_factor + sink_factor
    numerator = (
        cache_out.reshape(decode_row_count, QUERY_HEADS, HEAD_SIZE) * cache_factor[..., None]
        + own_factor[..., None] * row_own_values
    )
    return (
        (numerator / denominator[..., None])
        .reshape(decode_row_count, QUERY_HEADS * HEAD_SIZE)
        .astype(jnp.bfloat16)
    )

def layer_kernel(
    n,
    q_ref,
    kv_ref,
    branch_ref,
    sink_ref,
    residual_ref,
    gain_ref,
    ids_ref,
    codes_ref,
    cache_hbm,
    wo_hbm,
    wg_hbm,
    wu_hbm,
    wd_hbm,
    attended_ref,
    out_ref,
    cache,
    wo,
    hidden_t,
    OS,
    OR,
    TS,
    TR,
    osend,
    orecv,
    tsend,
    trecv,
    wg,
    wu,
    wd,
    X,
    act_ref,
    PS,
    CS,
    KEEP,
    YS,
    YR,
    ZS,
    ZR,
    wsem,
    xysend,
    xzsend,
    xmsend,
    xrecv,
    csend,
    crecv,
    ysend,
    yrecv,
    zsend,
    zrecv,
):
    rings = n // 2
    rows = residual_ref.shape[0]
    width = residual_ref.shape[1]
    half = X.shape[4]
    parts = rows // half
    experts = n
    a = lax.axis_index("att")
    e = lax.axis_index("exp")
    z = e // 2
    c = e % 2

    upper = z // 2
    twin = upper * 2 + 1 - z % 2
    near = 2 - upper
    far = 3 * (1 - upper)
    others = [twin, near, far]
    mate = {"exp": z * 2 + 1 - c}
    across = {"att": 1 - a}

    cache_load = pltpu.make_async_copy(cache_hbm, cache, wsem.at[3])
    cache_load.start()
    wo_load = pltpu.make_async_copy(wo_hbm, wo, wsem.at[4])
    wo_load.start()
    loads = [
        pltpu.make_async_copy(wg_hbm.at[0], wg, wsem.at[0]),
        pltpu.make_async_copy(wu_hbm.at[0], wu, wsem.at[1]),
        pltpu.make_async_copy(wd_hbm.at[0], wd, wsem.at[2]),
    ]
    for load in loads:
        load.start()

    barrier = pltpu.get_barrier_semaphore()
    for target in [mate, across] + [{"exp": chip * 2 + c} for chip in others]:
        pl.semaphore_signal(barrier, inc=1, device_id=target, device_id_type=MESH)
    eye = lax.broadcasted_iota(jnp.int32, (rows, rows), 0) == lax.broadcasted_iota(
        jnp.int32, (rows, rows), 1
    )

    per = QUERY_HEADS // KEY_VALUE_HEADS
    pair = 2 * HEAD_SIZE
    pairs = KEY_VALUE_HEADS // 2
    kv_width = KEY_VALUE_HEADS * HEAD_SIZE

    def span(h):
        return slice(h * half, (h + 1) * half)

    second_context = [
        jnp.concatenate([branch_ref[:, span(h)]] * per, axis=1) == 1 for h in range(parts)
    ]

    def transposed_queries(h, g2):
        start = pl.multiple_of(g2 * 2 * per * HEAD_SIZE, 128)
        block = q_ref[span(h), pl.ds(start, 2 * per * HEAD_SIZE)].astype(jnp.float32).T
        block = block * HEAD_SIZE ** (-0.5)

        def head(k):
            return block[k * HEAD_SIZE : (k + 1) * HEAD_SIZE]

        return [
            jnp.concatenate([head(j * per + m) for m in range(per)], axis=1) for j in range(2)
        ]

    def parts_copies(i):
        return (
            pltpu.make_async_remote_copy(
                src_ref=OS.at[i],
                dst_ref=OR.at[i],
                send_sem=osend.at[i],
                recv_sem=orecv.at[i],
                device_id=across,
                device_id_type=MESH,
            ),
            pltpu.make_async_remote_copy(
                src_ref=TS.at[i],
                dst_ref=TR.at[i],
                send_sem=tsend.at[i],
                recv_sem=trecv.at[i],
                device_id=across,
                device_id_type=MESH,
            ),
        )

    both_contexts = jnp.concatenate(second_context, axis=1)
    piece = per * half

    def send_parts(i):
        for copy in parts_copies(i):
            copy.start()

    def attend():
        @pl.loop(0, pairs)
        def _(g2):
            start = pl.multiple_of(g2 * 2 * per * HEAD_SIZE, 128)
            block = q_ref[:, pl.ds(start, 2 * per * HEAD_SIZE)].astype(jnp.float32).T
            block = block * HEAD_SIZE ** (-0.5)
            key_cols = pl.ds(pl.multiple_of(g2 * pair, 128), pair)
            value_cols = pl.ds(pl.multiple_of(kv_width + g2 * pair, 128), pair)
            keys = jnp.concatenate([cache[0, :, key_cols], cache[1, :, key_cols]], axis=1)
            values_t = [cache[k, :, value_cols].T for k in range(2)]
            for j in range(2):
                heads = [
                    block[(j * per + m) * HEAD_SIZE : (j * per + m + 1) * HEAD_SIZE]
                    for m in range(per)
                ]
                q = jnp.concatenate(
                    [head[:, span(h)] for h in range(parts) for head in heads], axis=1
                )
                none = jnp.zeros_like(q)
                first_q = jnp.where(both_contexts, 0.0, q)
                second_q = jnp.where(both_contexts, q, 0.0)
                stack = (
                    [first_q, none, second_q, none] if j == 0 else [none, first_q, none, second_q]
                )
                stacked = jnp.concatenate(stack, axis=0).astype(jnp.bfloat16)
                scores = jnp.dot(keys, stacked, preferred_element_type=jnp.float32)
                top = jnp.max(scores, axis=0, keepdims=True)
                weights = jnp.exp(scores - top)
                total = jnp.sum(weights, axis=0, keepdims=True)
                own_rows = slice(j * HEAD_SIZE, (j + 1) * HEAD_SIZE)
                values = jnp.concatenate([v[own_rows] for v in values_t], axis=0)
                out = jnp.dot(
                    values, weights.astype(jnp.bfloat16), preferred_element_type=jnp.float32
                )
                out = jnp.where(both_contexts, out[HEAD_SIZE:], out[:HEAD_SIZE])
                out = out.astype(jnp.bfloat16)
                for h in range(parts):
                    i = h * pairs + g2
                    own_cols = slice(h * piece, (h + 1) * piece)
                    OS[i, own_rows, :] = out[:, own_cols]
                    TS[i, 2 * j : 2 * j + 1, :] = top[:, own_cols]
                    TS[i, 2 * j + 1 : 2 * j + 2, :] = total[:, own_cols]

            @pl.when(g2 == 0)
            def _():
                pl.semaphore_wait(barrier, 2 + len(others))

            send_parts(g2)

            @pl.when(g2 == 1)
            def _():
                send_parts(pairs)

        for g2 in range(1, pairs):
            send_parts(pairs + g2)

    def project(h, start, stop):
        @pl.loop(start, stop)
        def _(g2):
            i = h * pairs + g2
            heads_t = transposed_queries(h, g2)
            key_cols = pl.ds(pl.multiple_of(g2 * pair, 128), pair)
            value_cols = pl.ds(pl.multiple_of(kv_width + g2 * pair, 128), pair)
            own_keys = kv_ref[span(h), key_cols].astype(jnp.float32).T
            own_values = kv_ref[span(h), value_cols].astype(jnp.float32).T
            for copy in parts_copies(i):
                copy.wait()
            mine, theirs = TS[i], TR[i]
            stacked = []
            for j in range(2):
                own_rows = slice(j * HEAD_SIZE, (j + 1) * HEAD_SIZE)
                own_key = jnp.concatenate([own_keys[own_rows]] * per, axis=1)
                own_value = jnp.concatenate([own_values[own_rows]] * per, axis=1)
                own_score = jnp.sum(heads_t[j] * own_key, axis=0, keepdims=True)
                sink = jnp.concatenate(
                    [
                        jnp.full((1, half), sink_ref[(g2 * 2 + j) * per + m])
                        for m in range(per)
                    ],
                    axis=1,
                )
                top_a, top_b = mine[2 * j : 2 * j + 1], theirs[2 * j : 2 * j + 1]
                peak = jnp.maximum(jnp.maximum(top_a, top_b), jnp.maximum(own_score, sink))
                factor_a = jnp.exp(top_a - peak)
                factor_b = jnp.exp(top_b - peak)
                own_factor = jnp.exp(own_score - peak)
                denominator = (
                    mine[2 * j + 1 : 2 * j + 2] * factor_a
                    + theirs[2 * j + 1 : 2 * j + 2] * factor_b
                    + own_factor
                    + jnp.exp(sink - peak)
                )
                out = (
                    OS[i, own_rows, :].astype(jnp.float32) * factor_a
                    + OR[i, own_rows, :].astype(jnp.float32) * factor_b
                    + own_factor * own_value
                ) / denominator
                stacked += [out[:, m * half : (m + 1) * half] for m in range(per)]
            attention_t = jnp.concatenate(stacked, axis=0).astype(jnp.bfloat16)
            cols = pl.ds(pl.multiple_of(g2 * 2 * per * HEAD_SIZE, 128), 2 * per * HEAD_SIZE)
            hidden_t[h] += jnp.dot(wo[:, cols], attention_t, preferred_element_type=jnp.float32)

    codes = codes_ref[...].astype(jnp.float32)
    codes = codes / jnp.sum(codes, axis=0, keepdims=True)
    row_of = lax.broadcasted_iota(jnp.int32, (experts, rows), 0)
    table = jnp.zeros((experts, rows), jnp.float32)
    for k in range(TOP):
        table += jnp.where(row_of == ids_ref[k : k + 1, :], codes[k : k + 1, :], 0.0)
    high = table.astype(jnp.bfloat16)
    low = (table - high.astype(jnp.float32)).astype(jnp.bfloat16)
    upright = lax.dot_general(
        eye.astype(jnp.bfloat16),
        jnp.concatenate([high, low], axis=0),
        NT,
        preferred_element_type=jnp.float32,
    )
    spare = X.shape[5] - width

    def normalise(h):
        hidden = hidden_t[h].T + residual_ref[span(h), :].astype(jnp.float32)
        attended_ref[span(h), :] = hidden.astype(jnp.bfloat16)
        squares = jnp.sum(hidden * hidden, axis=1, keepdims=True)
        first_part = squares.astype(jnp.bfloat16).astype(jnp.float32)
        second_part = (squares - first_part).astype(jnp.bfloat16).astype(jnp.float32)
        third_part = squares - first_part - second_part
        notes = jnp.concatenate(
            [
                upright[span(h)],
                first_part,
                second_part,
                third_part,
                jnp.zeros((half, spare - 2 * experts - 3), jnp.float32),
            ],
            axis=1,
        )
        scaled = hidden * gain_ref[...].astype(jnp.float32).reshape(1, width)
        X[a, c, z, h] = jnp.concatenate([scaled, notes], axis=1).astype(jnp.bfloat16)

    pending = []

    def push(index, target, sent):
        copy = pltpu.make_async_remote_copy(
            src_ref=X.at[index],
            dst_ref=X.at[index],
            send_sem=sent,
            recv_sem=xrecv.at[index],
            device_id=target,
            device_id_type=MESH,
        )
        return copy

    def arrived(side, core, chip, h):
        push((side, core, chip, h), mate, xmsend.at[0]).wait_recv()

    order = [z] + others

    def mate_copy(side, k, h):
        slot = (2 * k + h) * 2 + side
        return push(((a + side) % 2, c, order[k], h), mate, xmsend.at[slot])

    def across_copy(k, h):
        return push((a, c, order[k], h), across, xysend.at[2 * k + h])

    def along_copy(k, h):
        return push((a, c, z, h), {"exp": order[k] * 2 + c}, xzsend.at[2 * k + h])

    def relay_copy(h):
        return push((a, c, far, h), {"exp": twin * 2 + c}, xzsend.at[h])

    middle = (z == 1) | (z == 2)

    def along(h):
        @pl.when(middle)
        def _():
            along_copy(3, h).start()

        for k in (2, 1):
            along_copy(k, h).start()

    def came(k, h):
        arrived(a, c, order[k], h)
        across_copy(k, h).start()
        mate_copy(0, k, h).start()

    def came_far_middle(h):
        @pl.when(middle)
        def _():
            arrived(a, c, far, h)
            relay_copy(h).start()
            across_copy(3, h).start()
            mate_copy(0, 3, h).start()

    def came_far_end(h):
        @pl.when(jnp.logical_not(middle))
        def _():
            came(3, h)

    def crossed(k, h):
        arrived(1 - a, c, order[k], h)
        mate_copy(1, k, h).start()

    def mates(pieces):
        for k, h in pieces:
            for side in range(2):
                arrived(side, 1 - c, order[k], h)

    chunks = [[(k, h) for k in range(rings)] for h in range(parts)]

    def launch(h):
        across_copy(0, h).start()
        along(h)
        mate_copy(0, 0, h).start()

    count = n * half

    def tiles_of(total, tile):
        return [(start, min(tile, total - start)) for start in range(0, total, tile)]

    def prepare(pieces):
        sides = [
            jnp.concatenate(
                [X[side, core, order[k], h] for core in range(2) for k, h in pieces], axis=0
            )
            for side in range(2)
        ]
        x = jnp.concatenate([side[:, :width] for side in sides], axis=1)
        notes = [side[:, width:].astype(jnp.float32) for side in sides]
        lane = lax.broadcasted_iota(jnp.int32, notes[0].shape, 1)
        mine = (lane == e) | (lane == e + experts)
        share = jnp.sum(jnp.where(mine, notes[0], 0.0), axis=1, keepdims=True)
        sums = (lane >= 2 * experts) & (lane < 2 * experts + 3)
        squares = jnp.sum(
            jnp.where(sums, notes[0] + notes[1], 0.0), axis=1, keepdims=True
        )
        return x, share, lax.rsqrt(squares / (2 * width) + 1e-05)

    def first(x, inverse, start, size):
        cols = pl.ds(start, size)
        g = lax.dot_general(x, wg[cols, :], NT, preferred_element_type=jnp.float32)
        u = lax.dot_general(x, wu[cols, :], NT, preferred_element_type=jnp.float32)
        g = jnp.minimum(g * inverse, clamp_limit)
        u = jnp.clip(u * inverse, -clamp_limit, clamp_limit)
        act_ref[:, cols] = (g * jax.nn.sigmoid(1.702 * g) * (u + 1.0)).astype(jnp.bfloat16)

    lead = width % 128
    reach = width + lead

    def second(share, s):
        side = (1 - a) if s == 0 else a
        cols = pl.ds(pl.multiple_of(side * (width - lead), 128), reach)
        y = jnp.dot(act_ref[...], wd[:, cols], preferred_element_type=jnp.float32)
        y = jnp.where(side == 0, y[:, :width], y[:, lead:]) * share
        y = y.astype(jnp.bfloat16)
        for k in range(2):
            PS[s, k] = y[k * rings * half : (k + 1) * rings * half]

    def swap(g, s):
        copy = pltpu.make_async_remote_copy(
            src_ref=PS.at[s, 1 - c],
            dst_ref=CS.at[g, s],
            send_sem=csend.at[g, s],
            recv_sem=crecv.at[g, s],
            device_id=mate,
            device_id_type=MESH,
        )
        copy.start()
        return copy

    def crossing(g, p):
        mine = pl.ds(p * half, half)
        return pltpu.make_async_remote_copy(
            src_ref=YS.at[g, mine],
            dst_ref=YR.at[g, mine],
            send_sem=ysend.at[g, p],
            recv_sem=yrecv.at[g, p],
            device_id=across,
            device_id_type=MESH,
        )

    def cross_over(g):
        total = PS[0, c].astype(jnp.float32) + CS[g, 0].astype(jnp.float32)
        YS[g] = total.astype(jnp.bfloat16)
        for p in (3, 2, 1, 0):
            crossing(g, p).start()

    def keep(g):
        KEEP[g] = PS[1, c].astype(jnp.float32) + CS[g, 1].astype(jnp.float32)

    def merged(g, p):
        crossing(g, p).wait()
        mine = pl.ds(p * half, half)
        return KEEP[g, mine] + YR[g, mine].astype(jnp.float32)

    def delivery(g, p):
        k, h = chunks[g][p]
        return pltpu.make_async_remote_copy(
            src_ref=ZS.at[g, pl.ds(p * half, half)],
            dst_ref=ZR.at[h, z],
            send_sem=zsend.at[g, p],
            recv_sem=zrecv.at[h, z],
            device_id={"exp": order[k] * 2 + c},
            device_id_type=MESH,
        )

    def deliver(g, p):
        ZS[g, pl.ds(p * half, half)] = merged(g, p).astype(jnp.bfloat16)
        delivery(g, p).start()

    def finish(h):
        total = merged(h, 0)
        for k in (1, 2, 3):
            pltpu.make_async_remote_copy(
                src_ref=ZR.at[h, order[k]],
                dst_ref=ZR.at[h, order[k]],
                send_sem=zsend.at[0, 0],
                recv_sem=zrecv.at[h, order[k]],
                device_id=mate,
                device_id_type=MESH,
            ).wait_recv()
            total += ZR[h, order[k]].astype(jnp.float32)
        out_ref[h * half : (h + 1) * half, :] = total.astype(jnp.bfloat16)

    tiles = tiles_of(width, 512)
    cache_load.wait()
    attend()
    hidden_t[...] = jnp.zeros_like(hidden_t)
    wo_load.wait()
    project(0, 0, pairs)
    normalise(0)
    launch(0)
    project(1, 0, 3)
    came(1, 0)
    project(1, 3, pairs)
    normalise(1)
    launch(1)
    crossed(0, 0)
    came(2, 0)
    came_far_middle(0)
    crossed(1, 0)
    came_far_end(0)
    crossed(2, 0)
    came(1, 1)
    crossed(3, 0)
    mates(chunks[0])
    loads[0].wait()
    loads[1].wait()
    x, share, inverse = prepare(chunks[0])
    came(2, 1)
    came_far_middle(1)
    first(x, inverse, *tiles[0])
    crossed(0, 1)
    first(x, inverse, *tiles[1])
    came_far_end(1)
    crossed(1, 1)
    for tile in tiles[2:]:
        first(x, inverse, *tile)
    loads[2].wait()
    second(share, 0)
    swap_other = swap(0, 0)
    crossed(2, 1)
    swap_other.wait()
    cross_over(0)
    second(share, 1)
    swap_own = swap(0, 1)
    crossed(3, 1)
    swap_own.wait()
    keep(0)
    mates(chunks[1])
    x, share, inverse = prepare(chunks[1])
    first(x, inverse, *tiles[0])
    first(x, inverse, *tiles[1])
    deliver(0, 3)
    for tile in tiles[2:]:
        first(x, inverse, *tile)
    deliver(0, 2)
    second(share, 0)
    swap_other = swap(1, 0)
    deliver(0, 1)
    swap_other.wait()
    cross_over(1)
    second(share, 1)
    swap_own = swap(1, 1)
    swap_own.wait()
    keep(1)
    for p in (3, 2, 1):
        deliver(1, p)
    finish(0)
    finish(1)
    for k in range(rings):
        for h in range(parts):
            across_copy(k, h).wait_send()
            for side in range(2):
                mate_copy(side, k, h).wait_send()
    for h in range(parts):
        for k in (1, 2):
            along_copy(k, h).wait_send()

        @pl.when(middle)
        def _():
            along_copy(3, h).wait_send()
            relay_copy(h).wait_send()

    for g in range(2):
        for p in range(rings):
            if chunks[g][p][0]:
                delivery(g, p).wait_send()


def copy_kernel(first_ref, second_ref, first_out, second_out):
    first_out[...] = first_ref[...]
    second_out[...] = second_ref[...]


def copied(first, second):
    return pl.pallas_call(
        copy_kernel,
        out_shape=[
            jax.ShapeDtypeStruct(first.shape, first.dtype),
            jax.ShapeDtypeStruct(second.shape, second.dtype),
        ],
        in_specs=[pl.BlockSpec(memory_space=pltpu.VMEM)] * 2,
        out_specs=[pl.BlockSpec(memory_space=pltpu.VMEM)] * 2,
    )(first, second)


def layer(
    queries, row_key_value, cache, branch, sinks, w_out, residual, gain, expert_ids, weight_codes, w_gate, w_up, w_down
):
    n = lax.axis_size("exp")
    rings = n // 2
    rows, width = residual.shape
    per = QUERY_HEADS // KEY_VALUE_HEADS
    pairs = KEY_VALUE_HEADS // 2
    full = 2 * width
    half = rows // 2
    wide = -(-width // 128) * 128
    block = rings * half
    bf = jnp.bfloat16
    dma = pltpu.SemaphoreType.DMA
    return pl.pallas_call(
        functools.partial(layer_kernel, n),
        out_shape=[jax.ShapeDtypeStruct((rows, width), bf)] * 2,
        in_specs=[pl.BlockSpec(memory_space=pltpu.VMEM)] * 3
        + [pl.BlockSpec(memory_space=pltpu.SMEM)]
        + [pl.BlockSpec(memory_space=pltpu.VMEM)] * 4
        + [pl.BlockSpec(memory_space=pl.ANY)] * 5,
        out_specs=[pl.BlockSpec(memory_space=pltpu.VMEM)] * 2,
        scratch_shapes=[
            pltpu.VMEM(cache.shape, bf),
            pltpu.VMEM((width, QUERY_HEADS * HEAD_SIZE), bf),
            pltpu.VMEM((2, width, half), jnp.float32),
            pltpu.VMEM((2 * pairs, 2 * HEAD_SIZE, per * half), bf),
            pltpu.VMEM((2 * pairs, 2 * HEAD_SIZE, per * half), bf),
            pltpu.VMEM((2 * pairs, 4, per * half), jnp.float32),
            pltpu.VMEM((2 * pairs, 4, per * half), jnp.float32),
            dma((2 * pairs,)),
            dma((2 * pairs,)),
            dma((2 * pairs,)),
            dma((2 * pairs,)),
            pltpu.VMEM((width, full), bf),
            pltpu.VMEM((width, full), bf),
            pltpu.VMEM((width, full), bf),
            pltpu.VMEM((2, 2, rings, 2, half, wide), bf),
            pltpu.VMEM((n * half, width), bf),
            pltpu.VMEM((2, 2, block, width), bf),
            pltpu.VMEM((2, 2, block, width), bf),
            pltpu.VMEM((2, block, width), jnp.float32),
            pltpu.VMEM((2, block, width), bf),
            pltpu.VMEM((2, block, width), bf),
            pltpu.VMEM((2, block, width), bf),
            pltpu.VMEM((2, rings, half, width), bf),
            dma((5,)),
            dma((2 * rings,)),
            dma((2 * rings,)),
            dma((4 * rings,)),
            dma((2, 2, rings, 2)),
            dma((2, 2)),
            dma((2, 2)),
            dma((2, rings)),
            dma((2, rings)),
            dma((2, rings)),
            dma((2, rings)),
        ],
        compiler_params=pltpu.CompilerParams(
            collective_id=1, has_side_effects=True, vmem_limit_bytes=62 * 1024 * 1024
        ),
    )(
        queries,
        row_key_value,
        branch[None, :],
        sinks,
        residual,
        gain,
        expert_ids.T,
        weight_codes.T,
        cache,
        w_out.T,
        jnp.swapaxes(w_gate, 1, 2),
        jnp.swapaxes(w_up, 1, 2),
        w_down,
    )


def routed_experts(hidden, norm_gain, expert_ids, weight_codes, w_gate, w_up, w_down):
    decode_row_count = hidden.shape[0]
    squares = lax.psum(jnp.sum(hidden * hidden, axis=1), "att")
    inverse = lax.rsqrt(squares / D + 1e-05)
    normed = (hidden * inverse[:, None] * norm_gain.astype(jnp.float32)[None, :]).astype(
        jnp.bfloat16
    )
    local_experts = w_gate.shape[0]
    expert_count = local_experts * lax.axis_size("exp")
    capacity = min(decode_row_count, max(2, 2 * decode_row_count * TOP // expert_count))
    flat_ids = expert_ids.reshape(-1)
    expert_hits = (flat_ids[:, None] == jnp.arange(expert_count, dtype=jnp.int32)[None, :]).astype(
        jnp.int32
    )
    entries = flat_ids.shape[0]
    before = jnp.arange(entries)[:, None] > jnp.arange(entries)[None, :]
    earlier = jnp.dot(
        before.astype(jnp.bfloat16),
        expert_hits.astype(jnp.bfloat16),
        preferred_element_type=jnp.float32,
    ).astype(jnp.int32)
    position = jnp.sum(earlier * expert_hits, axis=1)
    slot_index = flat_ids * capacity + position
    placed = slot_index[None, :] == jnp.arange(expert_count * capacity, dtype=jnp.int32)[:, None]
    assign = jnp.any(placed.reshape(expert_count * capacity, decode_row_count, TOP), axis=2).astype(
        jnp.bfloat16
    )
    source_rows = lax.all_gather(normed, "att", axis=1, tiled=True)
    outgoing = jnp.dot(assign, source_rows, preferred_element_type=jnp.float32).astype(jnp.bfloat16)
    outgoing = outgoing.reshape(expert_count, capacity, -1)
    received = lax.all_to_all(outgoing, "exp", split_axis=0, concat_axis=0, tiled=True)
    senders = received.shape[0] // local_experts
    slot_count = received.shape[1]
    arranged = received.reshape(senders, local_experts, slot_count, received.shape[2])
    gate_sum = jnp.einsum("sekd,edf->sekf", arranged, w_gate, preferred_element_type=jnp.float32)
    up_sum = jnp.einsum("sekd,edf->sekf", arranged, w_up, preferred_element_type=jnp.float32)
    gate_sum = jnp.minimum(gate_sum, clamp_limit)
    up_sum = jnp.clip(up_sum, -clamp_limit, clamp_limit)
    active = (gate_sum * jax.nn.sigmoid(1.702 * gate_sum) * (up_sum + 1.0)).astype(jnp.bfloat16)
    partial_out = jnp.einsum("sekf,efd->sekd", active, w_down, preferred_element_type=jnp.float32)
    summed = lax.psum_scatter(
        partial_out.astype(jnp.bfloat16), "att", scatter_dimension=3, tiled=True
    )
    answer = lax.all_to_all(
        summed.reshape(senders * local_experts, slot_count, -1),
        "exp",
        split_axis=0,
        concat_axis=0,
        tiled=True,
    )
    flat_returned = answer.reshape(expert_count * capacity, -1)
    picked = flat_returned[slot_index].reshape(decode_row_count, TOP, -1).astype(jnp.float32)
    shares = weight_codes.astype(jnp.float32)
    shares = shares / jnp.sum(shares, axis=1, keepdims=True)
    mixture = jnp.sum(picked * shares[:, :, None], axis=1).astype(jnp.bfloat16)
    return mixture


def shards(
    queries,
    row_key_value,
    shared_context_cache,
    branch,
    sink_logits,
    w_out,
    residual,
    norm_gain,
    expert_ids,
    weight_codes,
    w_gate,
    w_up,
    w_down,
):
    near = lax.axis_size("att") == 2 and lax.axis_size("exp") == 8 and w_gate.shape[0] == 1
    if near:
        outputs = layer(
            queries,
            row_key_value,
            shared_context_cache,
            branch,
            sink_logits,
            w_out,
            residual,
            norm_gain,
            expert_ids,
            weight_codes,
            w_gate,
            w_up,
            w_down,
        )
        return copied(*outputs)
    decode_row_count = queries.shape[0]
    grouped_heads = queries.reshape(
        decode_row_count, KEY_VALUE_HEADS, QUERY_HEADS // KEY_VALUE_HEADS, HEAD_SIZE
    )
    partial_stats = local_partials(grouped_heads, shared_context_cache, branch)
    merged = combined_all(partial_stats, "att", merge_parts)
    attention = finish_attention(merged, grouped_heads, row_key_value, sink_logits)
    projected = jnp.dot(attention, w_out, preferred_element_type=jnp.float32)
    hidden = residual.astype(jnp.float32) + projected
    attended = hidden.astype(jnp.bfloat16)
    mixture = routed_experts(
        hidden, norm_gain, expert_ids, weight_codes, w_gate, w_up, w_down
    )
    return (attended, mixture)


def solution(mesh):
    placed = (
        P(("groups", "exp"), None),
        P(("groups", "exp"), None),
        P("groups", "att", None),
        P(("groups", "exp")),
        P(),
        P(None, "att"),
        P(("groups", "exp"), "att"),
        P("att"),
        P(("groups", "exp"), None),
        P(("groups", "exp"), None),
        P("exp", None, "att"),
        P("exp", None, "att"),
        P("exp", "att", None),
    )
    return jax.shard_map(
        shards,
        mesh=mesh,
        in_specs=placed,
        out_specs=(P(("groups", "exp"), "att"), P(("groups", "exp"), "att")),
        check_vma=False,
    )
```

```python
import functools

import jax
import jax.numpy as jnp
from jax import lax
from jax.experimental import pallas as pl
from jax.experimental.pallas import tpu as pltpu
from jax.sharding import PartitionSpec as P

D = 2880
QUERY_HEADS = 64
KEY_VALUE_HEADS = 8
HEAD_SIZE = 64
TOP = 4
SHARED_CONTEXTS = 2


MESH = pl.DeviceIdType.MESH
NT = (((1,), (1,)), ((), ()))
clamp_limit = 7.0


def combined_all(x, axis, combine):
    everything = jax.tree.map(
        lambda part, kind: lax.all_gather(part.astype(kind), axis),
        x,
        jax.tree.map(lambda a: jnp.bfloat16 if a.dtype == jnp.float32 else a.dtype, x),
    )

    def take(k):
        return jax.tree.map(lambda part, own: part[k].astype(own.dtype), everything, x)

    return lax.fori_loop(
        1, lax.axis_size(axis), lambda k, so_far: combine(so_far, take(k)), take(0)
    )


def merge_parts(first, second):
    first_max, first_total, first_out = first
    second_max, second_total, second_out = second
    joint_max = jnp.maximum(first_max, second_max)
    first_factor = jnp.exp(first_max - joint_max)
    second_factor = jnp.exp(second_max - joint_max)
    joint_total = first_total * first_factor + second_total * second_factor
    decode_row_count, head_count = first_max.shape
    joint_out = (
        first_out.reshape(decode_row_count, head_count, -1) * first_factor[:, :, None]
        + second_out.reshape(decode_row_count, head_count, -1) * second_factor[:, :, None]
    )
    return (joint_max, joint_total, joint_out.reshape(decode_row_count, -1))


def local_partials(grouped_heads, shared_context_cache, branch):
    decode_row_count = grouped_heads.shape[0]
    score_scale = HEAD_SIZE ** (-0.5)
    current = None
    for context_slot in range(SHARED_CONTEXTS):
        cached_key_block = shared_context_cache[
            context_slot, :, : KEY_VALUE_HEADS * HEAD_SIZE
        ].reshape(-1, KEY_VALUE_HEADS, HEAD_SIZE)
        cached_value_block = shared_context_cache[
            context_slot, :, KEY_VALUE_HEADS * HEAD_SIZE :
        ].reshape(-1, KEY_VALUE_HEADS, HEAD_SIZE)
        scores = (
            jnp.einsum(
                "rgqd,tgd->rgqt",
                grouped_heads,
                cached_key_block,
                preferred_element_type=jnp.float32,
            )
            * score_scale
        )
        local_max = jnp.max(scores, axis=-1)
        weights = jnp.exp(scores - local_max[..., None])
        local_total = jnp.sum(weights, axis=-1)
        local_out = jnp.einsum(
            "rgqt,tgd->rgqd",
            weights.astype(jnp.bfloat16),
            cached_value_block,
            preferred_element_type=jnp.float32,
        )
        if current is None:
            current = (local_max, local_total, local_out)
        else:
            chosen = branch == context_slot
            current = (
                jnp.where(chosen[:, None, None], local_max, current[0]),
                jnp.where(chosen[:, None, None], local_total, current[1]),
                jnp.where(chosen[:, None, None, None], local_out, current[2]),
            )
    return (
        current[0].reshape(decode_row_count, QUERY_HEADS),
        current[1].reshape(decode_row_count, QUERY_HEADS),
        current[2].reshape(decode_row_count, QUERY_HEADS * HEAD_SIZE),
    )


def finish_attention(merged, grouped_heads, row_key_value, sink_logits):
    decode_row_count = grouped_heads.shape[0]
    heads_per_group = QUERY_HEADS // KEY_VALUE_HEADS
    score_scale = HEAD_SIZE ** (-0.5)
    cache_max, cache_total, cache_out = merged
    row_own_keys = (
        row_key_value[:, : KEY_VALUE_HEADS * HEAD_SIZE]
        .reshape(decode_row_count, KEY_VALUE_HEADS, 1, HEAD_SIZE)
        .astype(jnp.float32)
    )
    row_own_values = (
        row_key_value[:, KEY_VALUE_HEADS * HEAD_SIZE :]
        .reshape(decode_row_count, KEY_VALUE_HEADS, 1, HEAD_SIZE)
        .astype(jnp.float32)
    )
    own_score = (
        jnp.sum(grouped_heads.astype(jnp.float32) * row_own_keys, axis=-1) * score_scale
    ).reshape(decode_row_count, QUERY_HEADS)
    row_own_values = jnp.broadcast_to(
        row_own_values, (decode_row_count, KEY_VALUE_HEADS, heads_per_group, HEAD_SIZE)
    ).reshape(decode_row_count, QUERY_HEADS, HEAD_SIZE)
    sink_row = sink_logits[None, :]
    peak = jnp.maximum(jnp.maximum(cache_max, own_score), sink_row)
    cache_factor = jnp.exp(cache_max - peak)
    own_factor = jnp.exp(own_score - peak)
    sink_factor = jnp.exp(sink_row - peak)
    denominator = cache_total * cache_factor + own_factor + sink_factor
    numerator = (
        cache_out.reshape(decode_row_count, QUERY_HEADS, HEAD_SIZE) * cache_factor[..., None]
        + own_factor[..., None] * row_own_values
    )
    return (
        (numerator / denominator[..., None])
        .reshape(decode_row_count, QUERY_HEADS * HEAD_SIZE)
        .astype(jnp.bfloat16)
    )

def layer_kernel(
    n,
    q_ref,
    kv_ref,
    branch_ref,
    sink_ref,
    residual_ref,
    gain_ref,
    ids_ref,
    codes_ref,
    cache_hbm,
    wo_hbm,
    wg_hbm,
    wu_hbm,
    wd_hbm,
    attended_ref,
    out_ref,
    cache,
    wo,
    hidden_t,
    OS,
    OR,
    TS,
    TR,
    osend,
    orecv,
    tsend,
    trecv,
    wg,
    wu,
    wd,
    X,
    act_ref,
    PS,
    CS,
    KEEP,
    YS,
    YR,
    ZS,
    ZR,
    wsem,
    xysend,
    xzsend,
    xmsend,
    xrecv,
    csend,
    crecv,
    ysend,
    yrecv,
    zsend,
    zrecv,
):
    rings = n // 2
    rows = residual_ref.shape[0]
    width = residual_ref.shape[1]
    half = X.shape[4]
    parts = rows // half
    experts = n
    a = lax.axis_index("att")
    e = lax.axis_index("exp")
    z = e // 2
    c = e % 2

    upper = z // 2
    twin = upper * 2 + 1 - z % 2
    near = 2 - upper
    far = 3 * (1 - upper)
    others = [twin, near, far]
    mate = {"exp": z * 2 + 1 - c}
    across = {"att": 1 - a}

    cache_load = pltpu.make_async_copy(cache_hbm, cache, wsem.at[3])
    cache_load.start()
    wo_load = pltpu.make_async_copy(wo_hbm, wo, wsem.at[4])
    wo_load.start()
    loads = [
        pltpu.make_async_copy(wg_hbm.at[0], wg, wsem.at[0]),
        pltpu.make_async_copy(wu_hbm.at[0], wu, wsem.at[1]),
        pltpu.make_async_copy(wd_hbm.at[0], wd, wsem.at[2]),
    ]
    for load in loads:
        load.start()

    barrier = pltpu.get_barrier_semaphore()
    for target in [mate, across] + [{"exp": chip * 2 + c} for chip in others]:
        pl.semaphore_signal(barrier, inc=1, device_id=target, device_id_type=MESH)
    eye = lax.broadcasted_iota(jnp.int32, (rows, rows), 0) == lax.broadcasted_iota(
        jnp.int32, (rows, rows), 1
    )

    per = QUERY_HEADS // KEY_VALUE_HEADS
    pair = 2 * HEAD_SIZE
    pairs = KEY_VALUE_HEADS // 2
    kv_width = KEY_VALUE_HEADS * HEAD_SIZE

    def span(h):
        return slice(h * half, (h + 1) * half)

    second_context = [
        jnp.concatenate([branch_ref[:, span(h)]] * per, axis=1) == 1 for h in range(parts)
    ]

    def transposed_queries(h, g2):
        start = pl.multiple_of(g2 * 2 * per * HEAD_SIZE, 128)
        block = q_ref[span(h), pl.ds(start, 2 * per * HEAD_SIZE)].astype(jnp.float32).T
        block = block * HEAD_SIZE ** (-0.5)

        def head(k):
            return block[k * HEAD_SIZE : (k + 1) * HEAD_SIZE]

        return [
            jnp.concatenate([head(j * per + m) for m in range(per)], axis=1) for j in range(2)
        ]

    def parts_copies(i):
        return (
            pltpu.make_async_remote_copy(
                src_ref=OS.at[i],
                dst_ref=OR.at[i],
                send_sem=osend.at[i],
                recv_sem=orecv.at[i],
                device_id=across,
                device_id_type=MESH,
            ),
            pltpu.make_async_remote_copy(
                src_ref=TS.at[i],
                dst_ref=TR.at[i],
                send_sem=tsend.at[i],
                recv_sem=trecv.at[i],
                device_id=across,
                device_id_type=MESH,
            ),
        )

    both_contexts = jnp.concatenate(second_context, axis=1)
    piece = per * half

    def send_parts(i):
        for copy in parts_copies(i):
            copy.start()

    def attend():
        @pl.loop(0, pairs)
        def _(g2):
            start = pl.multiple_of(g2 * 2 * per * HEAD_SIZE, 128)
            block = q_ref[:, pl.ds(start, 2 * per * HEAD_SIZE)].astype(jnp.float32).T
            block = block * HEAD_SIZE ** (-0.5)
            key_cols = pl.ds(pl.multiple_of(g2 * pair, 128), pair)
            value_cols = pl.ds(pl.multiple_of(kv_width + g2 * pair, 128), pair)
            keys = jnp.concatenate([cache[0, :, key_cols], cache[1, :, key_cols]], axis=1)
            values_t = [cache[k, :, value_cols].T for k in range(2)]
            for j in range(2):
                heads = [
                    block[(j * per + m) * HEAD_SIZE : (j * per + m + 1) * HEAD_SIZE]
                    for m in range(per)
                ]
                q = jnp.concatenate(
                    [head[:, span(h)] for h in range(parts) for head in heads], axis=1
                )
                none = jnp.zeros_like(q)
                first_q = jnp.where(both_contexts, 0.0, q)
                second_q = jnp.where(both_contexts, q, 0.0)
                stack = (
                    [first_q, none, second_q, none] if j == 0 else [none, first_q, none, second_q]
                )
                stacked = jnp.concatenate(stack, axis=0).astype(jnp.bfloat16)
                scores = jnp.dot(keys, stacked, preferred_element_type=jnp.float32)
                top = jnp.max(scores, axis=0, keepdims=True)
                weights = jnp.exp(scores - top)
                total = jnp.sum(weights, axis=0, keepdims=True)
                own_rows = slice(j * HEAD_SIZE, (j + 1) * HEAD_SIZE)
                values = jnp.concatenate([v[own_rows] for v in values_t], axis=0)
                out = jnp.dot(
                    values, weights.astype(jnp.bfloat16), preferred_element_type=jnp.float32
                )
                out = jnp.where(both_contexts, out[HEAD_SIZE:], out[:HEAD_SIZE])
                out = out.astype(jnp.bfloat16)
                for h in range(parts):
                    i = h * pairs + g2
                    own_cols = slice(h * piece, (h + 1) * piece)
                    OS[i, own_rows, :] = out[:, own_cols]
                    TS[i, 2 * j : 2 * j + 1, :] = top[:, own_cols]
                    TS[i, 2 * j + 1 : 2 * j + 2, :] = total[:, own_cols]

            @pl.when(g2 == 0)
            def _():
                pl.semaphore_wait(barrier, 2 + len(others))

            send_parts(g2)

            @pl.when(g2 == 1)
            def _():
                send_parts(pairs)

        for g2 in range(1, pairs):
            send_parts(pairs + g2)

    def project(h, start, stop):
        @pl.loop(start, stop)
        def _(g2):
            i = h * pairs + g2
            heads_t = transposed_queries(h, g2)
            key_cols = pl.ds(pl.multiple_of(g2 * pair, 128), pair)
            value_cols = pl.ds(pl.multiple_of(kv_width + g2 * pair, 128), pair)
            own_keys = kv_ref[span(h), key_cols].astype(jnp.float32).T
            own_values = kv_ref[span(h), value_cols].astype(jnp.float32).T
            for copy in parts_copies(i):
                copy.wait()
            mine, theirs = TS[i], TR[i]
            stacked = []
            for j in range(2):
                own_rows = slice(j * HEAD_SIZE, (j + 1) * HEAD_SIZE)
                own_key = jnp.concatenate([own_keys[own_rows]] * per, axis=1)
                own_value = jnp.concatenate([own_values[own_rows]] * per, axis=1)
                own_score = jnp.sum(heads_t[j] * own_key, axis=0, keepdims=True)
                sink = jnp.concatenate(
                    [
                        jnp.full((1, half), sink_ref[(g2 * 2 + j) * per + m])
                        for m in range(per)
                    ],
                    axis=1,
                )
                top_a, top_b = mine[2 * j : 2 * j + 1], theirs[2 * j : 2 * j + 1]
                peak = jnp.maximum(jnp.maximum(top_a, top_b), jnp.maximum(own_score, sink))
                factor_a = jnp.exp(top_a - peak)
                factor_b = jnp.exp(top_b - peak)
                own_factor = jnp.exp(own_score - peak)
                denominator = (
                    mine[2 * j + 1 : 2 * j + 2] * factor_a
                    + theirs[2 * j + 1 : 2 * j + 2] * factor_b
                    + own_factor
                    + jnp.exp(sink - peak)
                )
                out = (
                    OS[i, own_rows, :].astype(jnp.float32) * factor_a
                    + OR[i, own_rows, :].astype(jnp.float32) * factor_b
                    + own_factor * own_value
                ) / denominator
                stacked += [out[:, m * half : (m + 1) * half] for m in range(per)]
            attention_t = jnp.concatenate(stacked, axis=0).astype(jnp.bfloat16)
            cols = pl.ds(pl.multiple_of(g2 * 2 * per * HEAD_SIZE, 128), 2 * per * HEAD_SIZE)
            hidden_t[h] += jnp.dot(wo[:, cols], attention_t, preferred_element_type=jnp.float32)

    codes = codes_ref[...].astype(jnp.float32)
    codes = codes / jnp.sum(codes, axis=0, keepdims=True)
    row_of = lax.broadcasted_iota(jnp.int32, (experts, rows), 0)
    table = jnp.zeros((experts, rows), jnp.float32)
    for k in range(TOP):
        table += jnp.where(row_of == ids_ref[k : k + 1, :], codes[k : k + 1, :], 0.0)
    high = table.astype(jnp.bfloat16)
    low = (table - high.astype(jnp.float32)).astype(jnp.bfloat16)
    upright = lax.dot_general(
        eye.astype(jnp.bfloat16),
        jnp.concatenate([high, low], axis=0),
        NT,
        preferred_element_type=jnp.float32,
    )
    spare = X.shape[5] - width

    def normalise(h):
        hidden = hidden_t[h].T + residual_ref[span(h), :].astype(jnp.float32)
        attended_ref[span(h), :] = hidden.astype(jnp.bfloat16)
        squares = jnp.sum(hidden * hidden, axis=1, keepdims=True)
        first_part = squares.astype(jnp.bfloat16).astype(jnp.float32)
        second_part = (squares - first_part).astype(jnp.bfloat16).astype(jnp.float32)
        third_part = squares - first_part - second_part
        notes = jnp.concatenate(
            [
                upright[span(h)],
                first_part,
                second_part,
                third_part,
                jnp.zeros((half, spare - 2 * experts - 3), jnp.float32),
            ],
            axis=1,
        )
        scaled = hidden * gain_ref[...].astype(jnp.float32).reshape(1, width)
        X[a, c, z, h] = jnp.concatenate([scaled, notes], axis=1).astype(jnp.bfloat16)

    pending = []

    def push(index, target, sent):
        copy = pltpu.make_async_remote_copy(
            src_ref=X.at[index],
            dst_ref=X.at[index],
            send_sem=sent,
            recv_sem=xrecv.at[index],
            device_id=target,
            device_id_type=MESH,
        )
        return copy

    def arrived(side, core, chip, h):
        push((side, core, chip, h), mate, xmsend.at[0]).wait_recv()

    order = [z] + others

    def mate_copy(side, k, h):
        slot = (2 * k + h) * 2 + side
        return push(((a + side) % 2, c, order[k], h), mate, xmsend.at[slot])

    def across_copy(k, h):
        return push((a, c, order[k], h), across, xysend.at[2 * k + h])

    def along_copy(k, h):
        return push((a, c, z, h), {"exp": order[k] * 2 + c}, xzsend.at[2 * k + h])

    def relay_copy(h):
        return push((a, c, far, h), {"exp": twin * 2 + c}, xzsend.at[h])

    middle = (z == 1) | (z == 2)

    def along(h):
        along_copy(1, h).start()

        @pl.when(jnp.logical_not(middle))
        def _():
            along_copy(2, h).start()

    def along_middle(h):
        @pl.when(middle)
        def _():
            for k in (3, 2):
                along_copy(k, h).start()

    def came(k, h):
        arrived(a, c, order[k], h)
        across_copy(k, h).start()
        mate_copy(0, k, h).start()

    def came_far_middle(h):
        @pl.when(middle)
        def _():
            arrived(a, c, far, h)
            relay_copy(h).start()
            across_copy(3, h).start()
            mate_copy(0, 3, h).start()

    def came_far_end(h):
        @pl.when(jnp.logical_not(middle))
        def _():
            came(3, h)

    def crossed(k, h):
        arrived(1 - a, c, order[k], h)
        mate_copy(1, k, h).start()

    def mates(pieces):
        for k, h in pieces:
            for side in range(2):
                arrived(side, 1 - c, order[k], h)

    chunks = [[(k, h) for k in range(rings)] for h in range(parts)]

    def launch(h):
        along(h)
        mate_copy(0, 0, h).start()

    count = n * half

    def tiles_of(total, tile):
        return [(start, min(tile, total - start)) for start in range(0, total, tile)]

    def prepare(pieces):
        sides = [
            jnp.concatenate(
                [X[side, core, order[k], h] for core in range(2) for k, h in pieces], axis=0
            )
            for side in range(2)
        ]
        x = jnp.concatenate([side[:, :width] for side in sides], axis=1)
        notes = [side[:, width:].astype(jnp.float32) for side in sides]
        lane = lax.broadcasted_iota(jnp.int32, notes[0].shape, 1)
        mine = (lane == e) | (lane == e + experts)
        share = jnp.sum(jnp.where(mine, notes[0], 0.0), axis=1, keepdims=True)
        sums = (lane >= 2 * experts) & (lane < 2 * experts + 3)
        squares = jnp.sum(
            jnp.where(sums, notes[0] + notes[1], 0.0), axis=1, keepdims=True
        )
        return x, share, lax.rsqrt(squares / (2 * width) + 1e-05)

    def first(x, inverse, start, size):
        cols = pl.ds(start, size)
        g = lax.dot_general(x, wg[cols, :], NT, preferred_element_type=jnp.float32)
        u = lax.dot_general(x, wu[cols, :], NT, preferred_element_type=jnp.float32)
        g = jnp.minimum(g * inverse, clamp_limit)
        u = jnp.clip(u * inverse, -clamp_limit, clamp_limit)
        act_ref[:, cols] = (g * jax.nn.sigmoid(1.702 * g) * (u + 1.0)).astype(jnp.bfloat16)

    lead = width % 128
    reach = width + lead

    def second(share, s):
        side = (1 - a) if s == 0 else a
        cols = pl.ds(pl.multiple_of(side * (width - lead), 128), reach)
        y = jnp.dot(act_ref[...], wd[:, cols], preferred_element_type=jnp.float32)
        y = jnp.where(side == 0, y[:, :width], y[:, lead:]) * share
        y = y.astype(jnp.bfloat16)
        for k in range(2):
            PS[s, k] = y[k * rings * half : (k + 1) * rings * half]

    def swap(g, s):
        copy = pltpu.make_async_remote_copy(
            src_ref=PS.at[s, 1 - c],
            dst_ref=CS.at[g, s],
            send_sem=csend.at[g, s],
            recv_sem=crecv.at[g, s],
            device_id=mate,
            device_id_type=MESH,
        )
        copy.start()
        return copy

    def crossing(g, p):
        mine = pl.ds(p * half, half)
        return pltpu.make_async_remote_copy(
            src_ref=YS.at[g, mine],
            dst_ref=YR.at[g, mine],
            send_sem=ysend.at[g, p],
            recv_sem=yrecv.at[g, p],
            device_id=across,
            device_id_type=MESH,
        )

    def cross_over(g):
        total = PS[0, c].astype(jnp.float32) + CS[g, 0].astype(jnp.float32)
        YS[g] = total.astype(jnp.bfloat16)
        for p in (3, 2, 1, 0):
            crossing(g, p).start()

    def keep(g):
        KEEP[g] = PS[1, c].astype(jnp.float32) + CS[g, 1].astype(jnp.float32)

    def merged(g, p):
        crossing(g, p).wait()
        mine = pl.ds(p * half, half)
        return KEEP[g, mine] + YR[g, mine].astype(jnp.float32)

    def delivery(g, p):
        k, h = chunks[g][p]
        return pltpu.make_async_remote_copy(
            src_ref=ZS.at[g, pl.ds(p * half, half)],
            dst_ref=ZR.at[h, z],
            send_sem=zsend.at[g, p],
            recv_sem=zrecv.at[h, z],
            device_id={"exp": order[k] * 2 + c},
            device_id_type=MESH,
        )

    def deliver(g, p):
        ZS[g, pl.ds(p * half, half)] = merged(g, p).astype(jnp.bfloat16)
        delivery(g, p).start()

    def finish(h):
        total = merged(h, 0)
        for k in (1, 2, 3):
            pltpu.make_async_remote_copy(
                src_ref=ZR.at[h, order[k]],
                dst_ref=ZR.at[h, order[k]],
                send_sem=zsend.at[0, 0],
                recv_sem=zrecv.at[h, order[k]],
                device_id=mate,
                device_id_type=MESH,
            ).wait_recv()
            total += ZR[h, order[k]].astype(jnp.float32)
        out_ref[h * half : (h + 1) * half, :] = total.astype(jnp.bfloat16)

    tiles = tiles_of(width, 512)
    cache_load.wait()
    attend()
    hidden_t[...] = jnp.zeros_like(hidden_t)
    wo_load.wait()
    project(0, 0, pairs)
    normalise(0)
    across_copy(0, 0).start()
    launch(0)
    along_middle(0)
    project(1, 0, 3)
    came(1, 0)
    project(1, 3, pairs)
    came_far_middle(0)
    normalise(1)
    launch(1)
    along_middle(1)
    crossed(0, 0)
    came(2, 0)
    crossed(1, 0)
    came_far_end(0)
    across_copy(0, 1).start()
    crossed(2, 0)
    crossed(3, 0)
    came(1, 1)
    mates(chunks[0])
    loads[0].wait()
    loads[1].wait()
    x, share, inverse = prepare(chunks[0])
    first(x, inverse, *tiles[0])
    came_far_middle(1)
    came(2, 1)
    crossed(0, 1)
    first(x, inverse, *tiles[1])
    came_far_end(1)
    crossed(1, 1)
    for tile in tiles[2:]:
        first(x, inverse, *tile)
    loads[2].wait()
    second(share, 0)
    swap_other = swap(0, 0)
    crossed(2, 1)
    swap_other.wait()
    cross_over(0)
    second(share, 1)
    swap_own = swap(0, 1)
    crossed(3, 1)
    swap_own.wait()
    keep(0)
    mates(chunks[1])
    x, share, inverse = prepare(chunks[1])
    first(x, inverse, *tiles[0])
    first(x, inverse, *tiles[1])
    deliver(0, 3)
    for tile in tiles[2:]:
        first(x, inverse, *tile)
    deliver(0, 2)
    second(share, 0)
    swap_other = swap(1, 0)
    deliver(0, 1)
    swap_other.wait()
    cross_over(1)
    second(share, 1)
    swap_own = swap(1, 1)
    swap_own.wait()
    keep(1)
    for p in (3, 2, 1):
        deliver(1, p)
    finish(0)
    finish(1)
    for k in range(rings):
        for h in range(parts):
            across_copy(k, h).wait_send()
            for side in range(2):
                mate_copy(side, k, h).wait_send()
    for h in range(parts):
        for k in (1, 2):
            along_copy(k, h).wait_send()

        @pl.when(middle)
        def _():
            along_copy(3, h).wait_send()
            relay_copy(h).wait_send()

    for g in range(2):
        for p in range(rings):
            if chunks[g][p][0]:
                delivery(g, p).wait_send()


def copy_kernel(first_ref, second_ref, first_out, second_out):
    first_out[...] = first_ref[...]
    second_out[...] = second_ref[...]


def copied(first, second):
    return pl.pallas_call(
        copy_kernel,
        out_shape=[
            jax.ShapeDtypeStruct(first.shape, first.dtype),
            jax.ShapeDtypeStruct(second.shape, second.dtype),
        ],
        in_specs=[pl.BlockSpec(memory_space=pltpu.VMEM)] * 2,
        out_specs=[pl.BlockSpec(memory_space=pltpu.VMEM)] * 2,
    )(first, second)


def layer(
    queries, row_key_value, cache, branch, sinks, w_out, residual, gain, expert_ids, weight_codes, w_gate, w_up, w_down
):
    n = lax.axis_size("exp")
    rings = n // 2
    rows, width = residual.shape
    per = QUERY_HEADS // KEY_VALUE_HEADS
    pairs = KEY_VALUE_HEADS // 2
    full = 2 * width
    half = rows // 2
    wide = -(-width // 128) * 128
    block = rings * half
    bf = jnp.bfloat16
    dma = pltpu.SemaphoreType.DMA
    return pl.pallas_call(
        functools.partial(layer_kernel, n),
        out_shape=[jax.ShapeDtypeStruct((rows, width), bf)] * 2,
        in_specs=[pl.BlockSpec(memory_space=pltpu.VMEM)] * 3
        + [pl.BlockSpec(memory_space=pltpu.SMEM)]
        + [pl.BlockSpec(memory_space=pltpu.VMEM)] * 4
        + [pl.BlockSpec(memory_space=pl.ANY)] * 5,
        out_specs=[pl.BlockSpec(memory_space=pltpu.VMEM)] * 2,
        scratch_shapes=[
            pltpu.VMEM(cache.shape, bf),
            pltpu.VMEM((width, QUERY_HEADS * HEAD_SIZE), bf),
            pltpu.VMEM((2, width, half), jnp.float32),
            pltpu.VMEM((2 * pairs, 2 * HEAD_SIZE, per * half), bf),
            pltpu.VMEM((2 * pairs, 2 * HEAD_SIZE, per * half), bf),
            pltpu.VMEM((2 * pairs, 4, per * half), jnp.float32),
            pltpu.VMEM((2 * pairs, 4, per * half), jnp.float32),
            dma((2 * pairs,)),
            dma((2 * pairs,)),
            dma((2 * pairs,)),
            dma((2 * pairs,)),
            pltpu.VMEM((width, full), bf),
            pltpu.VMEM((width, full), bf),
            pltpu.VMEM((width, full), bf),
            pltpu.VMEM((2, 2, rings, 2, half, wide), bf),
            pltpu.VMEM((n * half, width), bf),
            pltpu.VMEM((2, 2, block, width), bf),
            pltpu.VMEM((2, 2, block, width), bf),
            pltpu.VMEM((2, block, width), jnp.float32),
            pltpu.VMEM((2, block, width), bf),
            pltpu.VMEM((2, block, width), bf),
            pltpu.VMEM((2, block, width), bf),
            pltpu.VMEM((2, rings, half, width), bf),
            dma((5,)),
            dma((2 * rings,)),
            dma((2 * rings,)),
            dma((4 * rings,)),
            dma((2, 2, rings, 2)),
            dma((2, 2)),
            dma((2, 2)),
            dma((2, rings)),
            dma((2, rings)),
            dma((2, rings)),
            dma((2, rings)),
        ],
        compiler_params=pltpu.CompilerParams(
            collective_id=1, has_side_effects=True, vmem_limit_bytes=62 * 1024 * 1024
        ),
    )(
        queries,
        row_key_value,
        branch[None, :],
        sinks,
        residual,
        gain,
        expert_ids.T,
        weight_codes.T,
        cache,
        w_out.T,
        jnp.swapaxes(w_gate, 1, 2),
        jnp.swapaxes(w_up, 1, 2),
        w_down,
    )


def routed_experts(hidden, norm_gain, expert_ids, weight_codes, w_gate, w_up, w_down):
    decode_row_count = hidden.shape[0]
    squares = lax.psum(jnp.sum(hidden * hidden, axis=1), "att")
    inverse = lax.rsqrt(squares / D + 1e-05)
    normed = (hidden * inverse[:, None] * norm_gain.astype(jnp.float32)[None, :]).astype(
        jnp.bfloat16
    )
    local_experts = w_gate.shape[0]
    expert_count = local_experts * lax.axis_size("exp")
    capacity = min(decode_row_count, max(2, 2 * decode_row_count * TOP // expert_count))
    flat_ids = expert_ids.reshape(-1)
    expert_hits = (flat_ids[:, None] == jnp.arange(expert_count, dtype=jnp.int32)[None, :]).astype(
        jnp.int32
    )
    entries = flat_ids.shape[0]
    before = jnp.arange(entries)[:, None] > jnp.arange(entries)[None, :]
    earlier = jnp.dot(
        before.astype(jnp.bfloat16),
        expert_hits.astype(jnp.bfloat16),
        preferred_element_type=jnp.float32,
    ).astype(jnp.int32)
    position = jnp.sum(earlier * expert_hits, axis=1)
    slot_index = flat_ids * capacity + position
    placed = slot_index[None, :] == jnp.arange(expert_count * capacity, dtype=jnp.int32)[:, None]
    assign = jnp.any(placed.reshape(expert_count * capacity, decode_row_count, TOP), axis=2).astype(
        jnp.bfloat16
    )
    source_rows = lax.all_gather(normed, "att", axis=1, tiled=True)
    outgoing = jnp.dot(assign, source_rows, preferred_element_type=jnp.float32).astype(jnp.bfloat16)
    outgoing = outgoing.reshape(expert_count, capacity, -1)
    received = lax.all_to_all(outgoing, "exp", split_axis=0, concat_axis=0, tiled=True)
    senders = received.shape[0] // local_experts
    slot_count = received.shape[1]
    arranged = received.reshape(senders, local_experts, slot_count, received.shape[2])
    gate_sum = jnp.einsum("sekd,edf->sekf", arranged, w_gate, preferred_element_type=jnp.float32)
    up_sum = jnp.einsum("sekd,edf->sekf", arranged, w_up, preferred_element_type=jnp.float32)
    gate_sum = jnp.minimum(gate_sum, clamp_limit)
    up_sum = jnp.clip(up_sum, -clamp_limit, clamp_limit)
    active = (gate_sum * jax.nn.sigmoid(1.702 * gate_sum) * (up_sum + 1.0)).astype(jnp.bfloat16)
    partial_out = jnp.einsum("sekf,efd->sekd", active, w_down, preferred_element_type=jnp.float32)
    summed = lax.psum_scatter(
        partial_out.astype(jnp.bfloat16), "att", scatter_dimension=3, tiled=True
    )
    answer = lax.all_to_all(
        summed.reshape(senders * local_experts, slot_count, -1),
        "exp",
        split_axis=0,
        concat_axis=0,
        tiled=True,
    )
    flat_returned = answer.reshape(expert_count * capacity, -1)
    picked = flat_returned[slot_index].reshape(decode_row_count, TOP, -1).astype(jnp.float32)
    shares = weight_codes.astype(jnp.float32)
    shares = shares / jnp.sum(shares, axis=1, keepdims=True)
    mixture = jnp.sum(picked * shares[:, :, None], axis=1).astype(jnp.bfloat16)
    return mixture


def shards(
    queries,
    row_key_value,
    shared_context_cache,
    branch,
    sink_logits,
    w_out,
    residual,
    norm_gain,
    expert_ids,
    weight_codes,
    w_gate,
    w_up,
    w_down,
):
    near = lax.axis_size("att") == 2 and lax.axis_size("exp") == 8 and w_gate.shape[0] == 1
    if near:
        outputs = layer(
            queries,
            row_key_value,
            shared_context_cache,
            branch,
            sink_logits,
            w_out,
            residual,
            norm_gain,
            expert_ids,
            weight_codes,
            w_gate,
            w_up,
            w_down,
        )
        return copied(*outputs)
    decode_row_count = queries.shape[0]
    grouped_heads = queries.reshape(
        decode_row_count, KEY_VALUE_HEADS, QUERY_HEADS // KEY_VALUE_HEADS, HEAD_SIZE
    )
    partial_stats = local_partials(grouped_heads, shared_context_cache, branch)
    merged = combined_all(partial_stats, "att", merge_parts)
    attention = finish_attention(merged, grouped_heads, row_key_value, sink_logits)
    projected = jnp.dot(attention, w_out, preferred_element_type=jnp.float32)
    hidden = residual.astype(jnp.float32) + projected
    attended = hidden.astype(jnp.bfloat16)
    mixture = routed_experts(
        hidden, norm_gain, expert_ids, weight_codes, w_gate, w_up, w_down
    )
    return (attended, mixture)


def solution(mesh):
    placed = (
        P(("groups", "exp"), None),
        P(("groups", "exp"), None),
        P("groups", "att", None),
        P(("groups", "exp")),
        P(),
        P(None, "att"),
        P(("groups", "exp"), "att"),
        P("att"),
        P(("groups", "exp"), None),
        P(("groups", "exp"), None),
        P("exp", None, "att"),
        P("exp", None, "att"),
        P("exp", "att", None),
    )
    return jax.shard_map(
        shards,
        mesh=mesh,
        in_specs=placed,
        out_specs=(P(("groups", "exp"), "att"), P(("groups", "exp"), "att")),
        check_vma=False,
    )
```

```python
import functools

import jax
import jax.numpy as jnp
from jax import lax
from jax.experimental import pallas as pl
from jax.experimental.pallas import tpu as pltpu
from jax.sharding import PartitionSpec as P

D = 2880
QUERY_HEADS = 64
KEY_VALUE_HEADS = 8
HEAD_SIZE = 64
TOP = 4
SHARED_CONTEXTS = 2


MESH = pl.DeviceIdType.MESH
NT = (((1,), (1,)), ((), ()))
clamp_limit = 7.0


def combined_all(x, axis, combine):
    everything = jax.tree.map(
        lambda part, kind: lax.all_gather(part.astype(kind), axis),
        x,
        jax.tree.map(lambda a: jnp.bfloat16 if a.dtype == jnp.float32 else a.dtype, x),
    )

    def take(k):
        return jax.tree.map(lambda part, own: part[k].astype(own.dtype), everything, x)

    return lax.fori_loop(
        1, lax.axis_size(axis), lambda k, so_far: combine(so_far, take(k)), take(0)
    )


def merge_parts(first, second):
    first_max, first_total, first_out = first
    second_max, second_total, second_out = second
    joint_max = jnp.maximum(first_max, second_max)
    first_factor = jnp.exp(first_max - joint_max)
    second_factor = jnp.exp(second_max - joint_max)
    joint_total = first_total * first_factor + second_total * second_factor
    decode_row_count, head_count = first_max.shape
    joint_out = (
        first_out.reshape(decode_row_count, head_count, -1) * first_factor[:, :, None]
        + second_out.reshape(decode_row_count, head_count, -1) * second_factor[:, :, None]
    )
    return (joint_max, joint_total, joint_out.reshape(decode_row_count, -1))


def local_partials(grouped_heads, shared_context_cache, branch):
    decode_row_count = grouped_heads.shape[0]
    score_scale = HEAD_SIZE ** (-0.5)
    current = None
    for context_slot in range(SHARED_CONTEXTS):
        cached_key_block = shared_context_cache[
            context_slot, :, : KEY_VALUE_HEADS * HEAD_SIZE
        ].reshape(-1, KEY_VALUE_HEADS, HEAD_SIZE)
        cached_value_block = shared_context_cache[
            context_slot, :, KEY_VALUE_HEADS * HEAD_SIZE :
        ].reshape(-1, KEY_VALUE_HEADS, HEAD_SIZE)
        scores = (
            jnp.einsum(
                "rgqd,tgd->rgqt",
                grouped_heads,
                cached_key_block,
                preferred_element_type=jnp.float32,
            )
            * score_scale
        )
        local_max = jnp.max(scores, axis=-1)
        weights = jnp.exp(scores - local_max[..., None])
        local_total = jnp.sum(weights, axis=-1)
        local_out = jnp.einsum(
            "rgqt,tgd->rgqd",
            weights.astype(jnp.bfloat16),
            cached_value_block,
            preferred_element_type=jnp.float32,
        )
        if current is None:
            current = (local_max, local_total, local_out)
        else:
            chosen = branch == context_slot
            current = (
                jnp.where(chosen[:, None, None], local_max, current[0]),
                jnp.where(chosen[:, None, None], local_total, current[1]),
                jnp.where(chosen[:, None, None, None], local_out, current[2]),
            )
    return (
        current[0].reshape(decode_row_count, QUERY_HEADS),
        current[1].reshape(decode_row_count, QUERY_HEADS),
        current[2].reshape(decode_row_count, QUERY_HEADS * HEAD_SIZE),
    )


def finish_attention(merged, grouped_heads, row_key_value, sink_logits):
    decode_row_count = grouped_heads.shape[0]
    heads_per_group = QUERY_HEADS // KEY_VALUE_HEADS
    score_scale = HEAD_SIZE ** (-0.5)
    cache_max, cache_total, cache_out = merged
    row_own_keys = (
        row_key_value[:, : KEY_VALUE_HEADS * HEAD_SIZE]
        .reshape(decode_row_count, KEY_VALUE_HEADS, 1, HEAD_SIZE)
        .astype(jnp.float32)
    )
    row_own_values = (
        row_key_value[:, KEY_VALUE_HEADS * HEAD_SIZE :]
        .reshape(decode_row_count, KEY_VALUE_HEADS, 1, HEAD_SIZE)
        .astype(jnp.float32)
    )
    own_score = (
        jnp.sum(grouped_heads.astype(jnp.float32) * row_own_keys, axis=-1) * score_scale
    ).reshape(decode_row_count, QUERY_HEADS)
    row_own_values = jnp.broadcast_to(
        row_own_values, (decode_row_count, KEY_VALUE_HEADS, heads_per_group, HEAD_SIZE)
    ).reshape(decode_row_count, QUERY_HEADS, HEAD_SIZE)
    sink_row = sink_logits[None, :]
    peak = jnp.maximum(jnp.maximum(cache_max, own_score), sink_row)
    cache_factor = jnp.exp(cache_max - peak)
    own_factor = jnp.exp(own_score - peak)
    sink_factor = jnp.exp(sink_row - peak)
    denominator = cache_total * cache_factor + own_factor + sink_factor
    numerator = (
        cache_out.reshape(decode_row_count, QUERY_HEADS, HEAD_SIZE) * cache_factor[..., None]
        + own_factor[..., None] * row_own_values
    )
    return (
        (numerator / denominator[..., None])
        .reshape(decode_row_count, QUERY_HEADS * HEAD_SIZE)
        .astype(jnp.bfloat16)
    )

def layer_kernel(
    n,
    q_ref,
    kv_ref,
    branch_ref,
    sink_ref,
    residual_ref,
    gain_ref,
    ids_ref,
    codes_ref,
    cache_hbm,
    wo_hbm,
    wg_hbm,
    wu_hbm,
    wd_hbm,
    attended_ref,
    out_ref,
    cache,
    wo,
    hidden_t,
    OS,
    OR,
    TS,
    TR,
    osend,
    orecv,
    tsend,
    trecv,
    wg,
    wu,
    wd,
    X,
    act_ref,
    PS,
    CS,
    KEEP,
    YS,
    YR,
    ZS,
    ZR,
    wsem,
    xysend,
    xzsend,
    xmsend,
    xrecv,
    csend,
    crecv,
    ysend,
    yrecv,
    zsend,
    zrecv,
):
    rings = n // 2
    rows = residual_ref.shape[0]
    width = residual_ref.shape[1]
    half = X.shape[4]
    parts = rows // half
    experts = n
    a = lax.axis_index("att")
    e = lax.axis_index("exp")
    z = e // 2
    c = e % 2

    upper = z // 2
    twin = upper * 2 + 1 - z % 2
    near = 2 - upper
    far = 3 * (1 - upper)
    others = [twin, near, far]
    mate = {"exp": z * 2 + 1 - c}
    across = {"att": 1 - a}

    cache_load = pltpu.make_async_copy(cache_hbm, cache, wsem.at[3])
    cache_load.start()
    wo_load = pltpu.make_async_copy(wo_hbm, wo, wsem.at[4])
    wo_load.start()
    loads = [
        pltpu.make_async_copy(wg_hbm.at[0], wg, wsem.at[0]),
        pltpu.make_async_copy(wu_hbm.at[0], wu, wsem.at[1]),
        pltpu.make_async_copy(wd_hbm.at[0], wd, wsem.at[2]),
    ]
    for load in loads:
        load.start()

    barrier = pltpu.get_barrier_semaphore()
    for target in [mate, across] + [{"exp": chip * 2 + c} for chip in others]:
        pl.semaphore_signal(barrier, inc=1, device_id=target, device_id_type=MESH)
    eye = lax.broadcasted_iota(jnp.int32, (rows, rows), 0) == lax.broadcasted_iota(
        jnp.int32, (rows, rows), 1
    )

    per = QUERY_HEADS // KEY_VALUE_HEADS
    pair = 2 * HEAD_SIZE
    pairs = KEY_VALUE_HEADS // 2
    kv_width = KEY_VALUE_HEADS * HEAD_SIZE

    def span(h):
        return slice(h * half, (h + 1) * half)

    second_context = [
        jnp.concatenate([branch_ref[:, span(h)]] * per, axis=1) == 1 for h in range(parts)
    ]

    def transposed_queries(h, g2):
        start = pl.multiple_of(g2 * 2 * per * HEAD_SIZE, 128)
        block = q_ref[span(h), pl.ds(start, 2 * per * HEAD_SIZE)].astype(jnp.float32).T
        block = block * HEAD_SIZE ** (-0.5)

        def head(k):
            return block[k * HEAD_SIZE : (k + 1) * HEAD_SIZE]

        return [
            jnp.concatenate([head(j * per + m) for m in range(per)], axis=1) for j in range(2)
        ]

    def parts_copies(i):
        return (
            pltpu.make_async_remote_copy(
                src_ref=OS.at[i],
                dst_ref=OR.at[i],
                send_sem=osend.at[i],
                recv_sem=orecv.at[i],
                device_id=across,
                device_id_type=MESH,
            ),
            pltpu.make_async_remote_copy(
                src_ref=TS.at[i],
                dst_ref=TR.at[i],
                send_sem=tsend.at[i],
                recv_sem=trecv.at[i],
                device_id=across,
                device_id_type=MESH,
            ),
        )

    both_contexts = jnp.concatenate(second_context, axis=1)
    piece = per * half

    def send_parts(i):
        for copy in parts_copies(i):
            copy.start()

    def attend():
        @pl.loop(0, pairs)
        def _(g2):
            start = pl.multiple_of(g2 * 2 * per * HEAD_SIZE, 128)
            block = q_ref[:, pl.ds(start, 2 * per * HEAD_SIZE)].astype(jnp.float32).T
            block = block * HEAD_SIZE ** (-0.5)
            key_cols = pl.ds(pl.multiple_of(g2 * pair, 128), pair)
            value_cols = pl.ds(pl.multiple_of(kv_width + g2 * pair, 128), pair)
            keys = jnp.concatenate([cache[0, :, key_cols], cache[1, :, key_cols]], axis=1)
            values_t = [cache[k, :, value_cols].T for k in range(2)]
            for j in range(2):
                heads = [
                    block[(j * per + m) * HEAD_SIZE : (j * per + m + 1) * HEAD_SIZE]
                    for m in range(per)
                ]
                q = jnp.concatenate(
                    [head[:, span(h)] for h in range(parts) for head in heads], axis=1
                )
                none = jnp.zeros_like(q)
                first_q = jnp.where(both_contexts, 0.0, q)
                second_q = jnp.where(both_contexts, q, 0.0)
                stack = (
                    [first_q, none, second_q, none] if j == 0 else [none, first_q, none, second_q]
                )
                stacked = jnp.concatenate(stack, axis=0).astype(jnp.bfloat16)
                scores = jnp.dot(keys, stacked, preferred_element_type=jnp.float32)
                top = jnp.max(scores, axis=0, keepdims=True)
                weights = jnp.exp(scores - top)
                total = jnp.sum(weights, axis=0, keepdims=True)
                own_rows = slice(j * HEAD_SIZE, (j + 1) * HEAD_SIZE)
                values = jnp.concatenate([v[own_rows] for v in values_t], axis=0)
                out = jnp.dot(
                    values, weights.astype(jnp.bfloat16), preferred_element_type=jnp.float32
                )
                out = jnp.where(both_contexts, out[HEAD_SIZE:], out[:HEAD_SIZE])
                out = out.astype(jnp.bfloat16)
                for h in range(parts):
                    i = h * pairs + g2
                    own_cols = slice(h * piece, (h + 1) * piece)
                    OS[i, own_rows, :] = out[:, own_cols]
                    TS[i, 2 * j : 2 * j + 1, :] = top[:, own_cols]
                    TS[i, 2 * j + 1 : 2 * j + 2, :] = total[:, own_cols]

            @pl.when(g2 == 0)
            def _():
                pl.semaphore_wait(barrier, 2 + len(others))

            send_parts(g2)

            @pl.when(g2 == 1)
            def _():
                send_parts(pairs)

        for g2 in range(1, pairs):
            send_parts(pairs + g2)

    def project(h, start, stop):
        @pl.loop(start, stop)
        def _(g2):
            i = h * pairs + g2
            heads_t = transposed_queries(h, g2)
            key_cols = pl.ds(pl.multiple_of(g2 * pair, 128), pair)
            value_cols = pl.ds(pl.multiple_of(kv_width + g2 * pair, 128), pair)
            own_keys = kv_ref[span(h), key_cols].astype(jnp.float32).T
            own_values = kv_ref[span(h), value_cols].astype(jnp.float32).T
            for copy in parts_copies(i):
                copy.wait()
            mine, theirs = TS[i], TR[i]
            stacked = []
            for j in range(2):
                own_rows = slice(j * HEAD_SIZE, (j + 1) * HEAD_SIZE)
                own_key = jnp.concatenate([own_keys[own_rows]] * per, axis=1)
                own_value = jnp.concatenate([own_values[own_rows]] * per, axis=1)
                own_score = jnp.sum(heads_t[j] * own_key, axis=0, keepdims=True)
                sink = jnp.concatenate(
                    [
                        jnp.full((1, half), sink_ref[(g2 * 2 + j) * per + m])
                        for m in range(per)
                    ],
                    axis=1,
                )
                top_a, top_b = mine[2 * j : 2 * j + 1], theirs[2 * j : 2 * j + 1]
                peak = jnp.maximum(jnp.maximum(top_a, top_b), jnp.maximum(own_score, sink))
                factor_a = jnp.exp(top_a - peak)
                factor_b = jnp.exp(top_b - peak)
                own_factor = jnp.exp(own_score - peak)
                denominator = (
                    mine[2 * j + 1 : 2 * j + 2] * factor_a
                    + theirs[2 * j + 1 : 2 * j + 2] * factor_b
                    + own_factor
                    + jnp.exp(sink - peak)
                )
                out = (
                    OS[i, own_rows, :].astype(jnp.float32) * factor_a
                    + OR[i, own_rows, :].astype(jnp.float32) * factor_b
                    + own_factor * own_value
                ) / denominator
                stacked += [out[:, m * half : (m + 1) * half] for m in range(per)]
            attention_t = jnp.concatenate(stacked, axis=0).astype(jnp.bfloat16)
            cols = pl.ds(pl.multiple_of(g2 * 2 * per * HEAD_SIZE, 128), 2 * per * HEAD_SIZE)
            hidden_t[h] += jnp.dot(wo[:, cols], attention_t, preferred_element_type=jnp.float32)

    codes = codes_ref[...].astype(jnp.float32)
    codes = codes / jnp.sum(codes, axis=0, keepdims=True)
    row_of = lax.broadcasted_iota(jnp.int32, (experts, rows), 0)
    table = jnp.zeros((experts, rows), jnp.float32)
    for k in range(TOP):
        table += jnp.where(row_of == ids_ref[k : k + 1, :], codes[k : k + 1, :], 0.0)
    high = table.astype(jnp.bfloat16)
    low = (table - high.astype(jnp.float32)).astype(jnp.bfloat16)
    upright = lax.dot_general(
        eye.astype(jnp.bfloat16),
        jnp.concatenate([high, low], axis=0),
        NT,
        preferred_element_type=jnp.float32,
    )
    spare = X.shape[5] - width

    def normalise(h):
        hidden = hidden_t[h].T + residual_ref[span(h), :].astype(jnp.float32)
        attended_ref[span(h), :] = hidden.astype(jnp.bfloat16)
        squares = jnp.sum(hidden * hidden, axis=1, keepdims=True)
        first_part = squares.astype(jnp.bfloat16).astype(jnp.float32)
        second_part = (squares - first_part).astype(jnp.bfloat16).astype(jnp.float32)
        third_part = squares - first_part - second_part
        notes = jnp.concatenate(
            [
                upright[span(h)],
                first_part,
                second_part,
                third_part,
                jnp.zeros((half, spare - 2 * experts - 3), jnp.float32),
            ],
            axis=1,
        )
        scaled = hidden * gain_ref[...].astype(jnp.float32).reshape(1, width)
        X[a, c, z, h] = jnp.concatenate([scaled, notes], axis=1).astype(jnp.bfloat16)

    pending = []

    def push(index, target, sent):
        copy = pltpu.make_async_remote_copy(
            src_ref=X.at[index],
            dst_ref=X.at[index],
            send_sem=sent,
            recv_sem=xrecv.at[index],
            device_id=target,
            device_id_type=MESH,
        )
        return copy

    def arrived(side, core, chip, h):
        push((side, core, chip, h), mate, xmsend.at[0]).wait_recv()

    order = [z] + others

    def mate_copy(side, k, h):
        slot = (2 * k + h) * 2 + side
        return push(((a + side) % 2, c, order[k], h), mate, xmsend.at[slot])

    def across_copy(k, h):
        return push((a, c, order[k], h), across, xysend.at[2 * k + h])

    def along_copy(k, h):
        return push((a, c, z, h), {"exp": order[k] * 2 + c}, xzsend.at[2 * k + h])

    def relay_copy(h):
        return push((a, c, far, h), {"exp": twin * 2 + c}, xzsend.at[h])

    middle = (z == 1) | (z == 2)

    def along(h):
        along_copy(1, h).start()

        @pl.when(jnp.logical_not(middle))
        def _():
            along_copy(2, h).start()

    def along_middle(h):
        @pl.when(middle)
        def _():
            for k in (3, 2):
                along_copy(k, h).start()

    def came(k, h):
        arrived(a, c, order[k], h)
        across_copy(k, h).start()
        mate_copy(0, k, h).start()

    def came_far_middle(h):
        @pl.when(middle)
        def _():
            arrived(a, c, far, h)
            relay_copy(h).start()
            across_copy(3, h).start()
            mate_copy(0, 3, h).start()

    def came_far_end(h):
        @pl.when(jnp.logical_not(middle))
        def _():
            came(3, h)

    def crossed(k, h):
        arrived(1 - a, c, order[k], h)
        mate_copy(1, k, h).start()

    def mates(pieces):
        for k, h in pieces:
            for side in range(2):
                arrived(side, 1 - c, order[k], h)

    chunks = [[(k, h) for k in range(rings)] for h in range(parts)]

    def launch(h):
        along(h)
        mate_copy(0, 0, h).start()

    count = n * half

    def tiles_of(total, tile):
        return [(start, min(tile, total - start)) for start in range(0, total, tile)]

    def prepare(pieces):
        sides = [
            jnp.concatenate(
                [X[side, core, order[k], h] for core in range(2) for k, h in pieces], axis=0
            )
            for side in range(2)
        ]
        x = jnp.concatenate([side[:, :width] for side in sides], axis=1)
        notes = [side[:, width:].astype(jnp.float32) for side in sides]
        lane = lax.broadcasted_iota(jnp.int32, notes[0].shape, 1)
        mine = (lane == e) | (lane == e + experts)
        share = jnp.sum(jnp.where(mine, notes[0], 0.0), axis=1, keepdims=True)
        sums = (lane >= 2 * experts) & (lane < 2 * experts + 3)
        squares = jnp.sum(
            jnp.where(sums, notes[0] + notes[1], 0.0), axis=1, keepdims=True
        )
        return x, share, lax.rsqrt(squares / (2 * width) + 1e-05)

    def first(x, inverse, start, size):
        cols = pl.ds(start, size)
        g = lax.dot_general(x, wg[cols, :], NT, preferred_element_type=jnp.float32)
        u = lax.dot_general(x, wu[cols, :], NT, preferred_element_type=jnp.float32)
        g = jnp.minimum(g * inverse, clamp_limit)
        u = jnp.clip(u * inverse, -clamp_limit, clamp_limit)
        act_ref[:, cols] = (g * jax.nn.sigmoid(1.702 * g) * (u + 1.0)).astype(jnp.bfloat16)

    lead = width % 128
    reach = width + lead

    def second(share, s):
        side = (1 - a) if s == 0 else a
        cols = pl.ds(pl.multiple_of(side * (width - lead), 128), reach)
        y = jnp.dot(act_ref[...], wd[:, cols], preferred_element_type=jnp.float32)
        y = jnp.where(side == 0, y[:, :width], y[:, lead:]) * share
        y = y.astype(jnp.bfloat16)
        for k in range(2):
            PS[s, k] = y[k * rings * half : (k + 1) * rings * half]

    def swap(g, s):
        copy = pltpu.make_async_remote_copy(
            src_ref=PS.at[s, 1 - c],
            dst_ref=CS.at[g, s],
            send_sem=csend.at[g, s],
            recv_sem=crecv.at[g, s],
            device_id=mate,
            device_id_type=MESH,
        )
        copy.start()
        return copy

    sub = half // 2
    subs = range(half // sub)

    def crossing(g, p, q):
        mine = pl.ds(p * half + q * sub, sub)
        return pltpu.make_async_remote_copy(
            src_ref=YS.at[g, mine],
            dst_ref=YR.at[g, mine],
            send_sem=ysend.at[g, 2 * p + q],
            recv_sem=yrecv.at[g, 2 * p + q],
            device_id=across,
            device_id_type=MESH,
        )

    def cross_over(g):
        total = PS[0, c].astype(jnp.float32) + CS[g, 0].astype(jnp.float32)
        YS[g] = total.astype(jnp.bfloat16)
        for p in (3, 2, 1, 0):
            for q in subs:
                crossing(g, p, q).start()

    def keep(g):
        KEEP[g] = PS[1, c].astype(jnp.float32) + CS[g, 1].astype(jnp.float32)

    def merged(g, p, q):
        crossing(g, p, q).wait()
        mine = pl.ds(p * half + q * sub, sub)
        return KEEP[g, mine] + YR[g, mine].astype(jnp.float32)

    def delivery(g, p, q):
        k, h = chunks[g][p]
        return pltpu.make_async_remote_copy(
            src_ref=ZS.at[g, pl.ds(p * half + q * sub, sub)],
            dst_ref=ZR.at[h, z, pl.ds(q * sub, sub)],
            send_sem=zsend.at[g, 2 * p + q],
            recv_sem=zrecv.at[h, z, q],
            device_id={"exp": order[k] * 2 + c},
            device_id_type=MESH,
        )

    def deliver(g, p):
        for q in subs:
            ZS[g, pl.ds(p * half + q * sub, sub)] = merged(g, p, q).astype(jnp.bfloat16)
            delivery(g, p, q).start()

    def finish(h):
        for q in subs:
            mine = pl.ds(q * sub, sub)
            total = merged(h, 0, q)
            for k in (1, 2, 3):
                pltpu.make_async_remote_copy(
                    src_ref=ZR.at[h, order[k], mine],
                    dst_ref=ZR.at[h, order[k], mine],
                    send_sem=zsend.at[0, 0],
                    recv_sem=zrecv.at[h, order[k], q],
                    device_id=mate,
                    device_id_type=MESH,
                ).wait_recv()
                total += ZR[h, order[k], mine].astype(jnp.float32)
            start = h * half + q * sub
            out_ref[start : start + sub, :] = total.astype(jnp.bfloat16)

    tiles = tiles_of(width, 512)
    cache_load.wait()
    attend()
    hidden_t[...] = jnp.zeros_like(hidden_t)
    wo_load.wait()
    project(0, 0, pairs)
    normalise(0)
    across_copy(0, 0).start()
    launch(0)
    along_middle(0)
    project(1, 0, 3)
    came(1, 0)
    project(1, 3, pairs)
    came_far_middle(0)
    normalise(1)
    launch(1)
    along_middle(1)
    crossed(0, 0)
    came(2, 0)
    crossed(1, 0)
    came_far_end(0)
    across_copy(0, 1).start()
    crossed(2, 0)
    crossed(3, 0)
    came(1, 1)
    mates(chunks[0])
    loads[0].wait()
    loads[1].wait()
    x, share, inverse = prepare(chunks[0])
    first(x, inverse, *tiles[0])
    came_far_middle(1)
    came(2, 1)
    crossed(0, 1)
    first(x, inverse, *tiles[1])
    came_far_end(1)
    crossed(1, 1)
    for tile in tiles[2:]:
        first(x, inverse, *tile)
    loads[2].wait()
    second(share, 0)
    swap_other = swap(0, 0)
    crossed(2, 1)
    second(share, 1)
    swap_own = swap(0, 1)
    swap_other.wait()
    cross_over(0)
    crossed(3, 1)
    mates(chunks[1])
    x, share, inverse = prepare(chunks[1])
    first(x, inverse, *tiles[0])
    swap_own.wait()
    keep(0)
    first(x, inverse, *tiles[1])
    deliver(0, 3)
    for tile in tiles[2:]:
        first(x, inverse, *tile)
    deliver(0, 2)
    second(share, 0)
    swap_other = swap(1, 0)
    deliver(0, 1)
    swap_other.wait()
    cross_over(1)
    second(share, 1)
    swap_own = swap(1, 1)
    swap_own.wait()
    keep(1)
    for p in (3, 2, 1):
        deliver(1, p)
    finish(0)
    finish(1)
    for k in range(rings):
        for h in range(parts):
            across_copy(k, h).wait_send()
            for side in range(2):
                mate_copy(side, k, h).wait_send()
    for h in range(parts):
        for k in (1, 2):
            along_copy(k, h).wait_send()

        @pl.when(middle)
        def _():
            along_copy(3, h).wait_send()
            relay_copy(h).wait_send()

    for g in range(2):
        for p in range(rings):
            if chunks[g][p][0]:
                for q in subs:
                    delivery(g, p, q).wait_send()


def copy_kernel(first_ref, second_ref, first_out, second_out):
    first_out[...] = first_ref[...]
    second_out[...] = second_ref[...]


def copied(first, second):
    return pl.pallas_call(
        copy_kernel,
        out_shape=[
            jax.ShapeDtypeStruct(first.shape, first.dtype),
            jax.ShapeDtypeStruct(second.shape, second.dtype),
        ],
        in_specs=[pl.BlockSpec(memory_space=pltpu.VMEM)] * 2,
        out_specs=[pl.BlockSpec(memory_space=pltpu.VMEM)] * 2,
    )(first, second)


def layer(
    queries, row_key_value, cache, branch, sinks, w_out, residual, gain, expert_ids, weight_codes, w_gate, w_up, w_down
):
    n = lax.axis_size("exp")
    rings = n // 2
    rows, width = residual.shape
    per = QUERY_HEADS // KEY_VALUE_HEADS
    pairs = KEY_VALUE_HEADS // 2
    full = 2 * width
    half = rows // 2
    wide = -(-width // 128) * 128
    block = rings * half
    bf = jnp.bfloat16
    dma = pltpu.SemaphoreType.DMA
    return pl.pallas_call(
        functools.partial(layer_kernel, n),
        out_shape=[jax.ShapeDtypeStruct((rows, width), bf)] * 2,
        in_specs=[pl.BlockSpec(memory_space=pltpu.VMEM)] * 3
        + [pl.BlockSpec(memory_space=pltpu.SMEM)]
        + [pl.BlockSpec(memory_space=pltpu.VMEM)] * 4
        + [pl.BlockSpec(memory_space=pl.ANY)] * 5,
        out_specs=[pl.BlockSpec(memory_space=pltpu.VMEM)] * 2,
        scratch_shapes=[
            pltpu.VMEM(cache.shape, bf),
            pltpu.VMEM((width, QUERY_HEADS * HEAD_SIZE), bf),
            pltpu.VMEM((2, width, half), jnp.float32),
            pltpu.VMEM((2 * pairs, 2 * HEAD_SIZE, per * half), bf),
            pltpu.VMEM((2 * pairs, 2 * HEAD_SIZE, per * half), bf),
            pltpu.VMEM((2 * pairs, 4, per * half), jnp.float32),
            pltpu.VMEM((2 * pairs, 4, per * half), jnp.float32),
            dma((2 * pairs,)),
            dma((2 * pairs,)),
            dma((2 * pairs,)),
            dma((2 * pairs,)),
            pltpu.VMEM((width, full), bf),
            pltpu.VMEM((width, full), bf),
            pltpu.VMEM((width, full), bf),
            pltpu.VMEM((2, 2, rings, 2, half, wide), bf),
            pltpu.VMEM((n * half, width), bf),
            pltpu.VMEM((2, 2, block, width), bf),
            pltpu.VMEM((2, 2, block, width), bf),
            pltpu.VMEM((2, block, width), jnp.float32),
            pltpu.VMEM((2, block, width), bf),
            pltpu.VMEM((2, block, width), bf),
            pltpu.VMEM((2, block, width), bf),
            pltpu.VMEM((2, rings, half, width), bf),
            dma((5,)),
            dma((2 * rings,)),
            dma((2 * rings,)),
            dma((4 * rings,)),
            dma((2, 2, rings, 2)),
            dma((2, 2)),
            dma((2, 2)),
            dma((2, 2 * rings)),
            dma((2, 2 * rings)),
            dma((2, 2 * rings)),
            dma((2, rings, 2)),
        ],
        compiler_params=pltpu.CompilerParams(
            collective_id=1, has_side_effects=True, vmem_limit_bytes=62 * 1024 * 1024
        ),
    )(
        queries,
        row_key_value,
        branch[None, :],
        sinks,
        residual,
        gain,
        expert_ids.T,
        weight_codes.T,
        cache,
        w_out.T,
        jnp.swapaxes(w_gate, 1, 2),
        jnp.swapaxes(w_up, 1, 2),
        w_down,
    )


def routed_experts(hidden, norm_gain, expert_ids, weight_codes, w_gate, w_up, w_down):
    decode_row_count = hidden.shape[0]
    squares = lax.psum(jnp.sum(hidden * hidden, axis=1), "att")
    inverse = lax.rsqrt(squares / D + 1e-05)
    normed = (hidden * inverse[:, None] * norm_gain.astype(jnp.float32)[None, :]).astype(
        jnp.bfloat16
    )
    local_experts = w_gate.shape[0]
    expert_count = local_experts * lax.axis_size("exp")
    capacity = min(decode_row_count, max(2, 2 * decode_row_count * TOP // expert_count))
    flat_ids = expert_ids.reshape(-1)
    expert_hits = (flat_ids[:, None] == jnp.arange(expert_count, dtype=jnp.int32)[None, :]).astype(
        jnp.int32
    )
    entries = flat_ids.shape[0]
    before = jnp.arange(entries)[:, None] > jnp.arange(entries)[None, :]
    earlier = jnp.dot(
        before.astype(jnp.bfloat16),
        expert_hits.astype(jnp.bfloat16),
        preferred_element_type=jnp.float32,
    ).astype(jnp.int32)
    position = jnp.sum(earlier * expert_hits, axis=1)
    slot_index = flat_ids * capacity + position
    placed = slot_index[None, :] == jnp.arange(expert_count * capacity, dtype=jnp.int32)[:, None]
    assign = jnp.any(placed.reshape(expert_count * capacity, decode_row_count, TOP), axis=2).astype(
        jnp.bfloat16
    )
    source_rows = lax.all_gather(normed, "att", axis=1, tiled=True)
    outgoing = jnp.dot(assign, source_rows, preferred_element_type=jnp.float32).astype(jnp.bfloat16)
    outgoing = outgoing.reshape(expert_count, capacity, -1)
    received = lax.all_to_all(outgoing, "exp", split_axis=0, concat_axis=0, tiled=True)
    senders = received.shape[0] // local_experts
    slot_count = received.shape[1]
    arranged = received.reshape(senders, local_experts, slot_count, received.shape[2])
    gate_sum = jnp.einsum("sekd,edf->sekf", arranged, w_gate, preferred_element_type=jnp.float32)
    up_sum = jnp.einsum("sekd,edf->sekf", arranged, w_up, preferred_element_type=jnp.float32)
    gate_sum = jnp.minimum(gate_sum, clamp_limit)
    up_sum = jnp.clip(up_sum, -clamp_limit, clamp_limit)
    active = (gate_sum * jax.nn.sigmoid(1.702 * gate_sum) * (up_sum + 1.0)).astype(jnp.bfloat16)
    partial_out = jnp.einsum("sekf,efd->sekd", active, w_down, preferred_element_type=jnp.float32)
    summed = lax.psum_scatter(
        partial_out.astype(jnp.bfloat16), "att", scatter_dimension=3, tiled=True
    )
    answer = lax.all_to_all(
        summed.reshape(senders * local_experts, slot_count, -1),
        "exp",
        split_axis=0,
        concat_axis=0,
        tiled=True,
    )
    flat_returned = answer.reshape(expert_count * capacity, -1)
    picked = flat_returned[slot_index].reshape(decode_row_count, TOP, -1).astype(jnp.float32)
    shares = weight_codes.astype(jnp.float32)
    shares = shares / jnp.sum(shares, axis=1, keepdims=True)
    mixture = jnp.sum(picked * shares[:, :, None], axis=1).astype(jnp.bfloat16)
    return mixture


def shards(
    queries,
    row_key_value,
    shared_context_cache,
    branch,
    sink_logits,
    w_out,
    residual,
    norm_gain,
    expert_ids,
    weight_codes,
    w_gate,
    w_up,
    w_down,
):
    near = lax.axis_size("att") == 2 and lax.axis_size("exp") == 8 and w_gate.shape[0] == 1
    if near:
        outputs = layer(
            queries,
            row_key_value,
            shared_context_cache,
            branch,
            sink_logits,
            w_out,
            residual,
            norm_gain,
            expert_ids,
            weight_codes,
            w_gate,
            w_up,
            w_down,
        )
        return copied(*outputs)
    decode_row_count = queries.shape[0]
    grouped_heads = queries.reshape(
        decode_row_count, KEY_VALUE_HEADS, QUERY_HEADS // KEY_VALUE_HEADS, HEAD_SIZE
    )
    partial_stats = local_partials(grouped_heads, shared_context_cache, branch)
    merged = combined_all(partial_stats, "att", merge_parts)
    attention = finish_attention(merged, grouped_heads, row_key_value, sink_logits)
    projected = jnp.dot(attention, w_out, preferred_element_type=jnp.float32)
    hidden = residual.astype(jnp.float32) + projected
    attended = hidden.astype(jnp.bfloat16)
    mixture = routed_experts(
        hidden, norm_gain, expert_ids, weight_codes, w_gate, w_up, w_down
    )
    return (attended, mixture)


def solution(mesh):
    placed = (
        P(("groups", "exp"), None),
        P(("groups", "exp"), None),
        P("groups", "att", None),
        P(("groups", "exp")),
        P(),
        P(None, "att"),
        P(("groups", "exp"), "att"),
        P("att"),
        P(("groups", "exp"), None),
        P(("groups", "exp"), None),
        P("exp", None, "att"),
        P("exp", None, "att"),
        P("exp", "att", None),
    )
    return jax.shard_map(
        shards,
        mesh=mesh,
        in_specs=placed,
        out_specs=(P(("groups", "exp"), "att"), P(("groups", "exp"), "att")),
        check_vma=False,
    )
```
